256 devices in a mesh: lat: 16 (over x, z_hi, core), tm: 16 (over y, z_lo).
Axes of the slice: x: 4, y: 4, z: 8 (z_hi: 2, z_lo: 4; z = z_hi * 4 + z_lo), core: 2. Of those that a mesh axis runs over, the one named last changes fastest.
Arguments:
- data: float32 [8, 256, 92160], P(None, 'tm', 'lat'), may hold values from -6 to 6
- space_init: float32 [32, 92160], P(None, 'lat'), may hold values from -0.01953125 to 0.01953125
- time_init: float32 [32, 256], P(None, 'tm'), may hold values from -6 to 6
- variable_factor: float32 [8, 32], replicated, may hold values from -2 to 2
- neighbours: int32 [4, 92160], P(None, 'lat'), may hold values from -1 to 92159, as said below
Outputs:
- time_factor: float32 [32, 256], P(None, 'tm')
- space_factor: float32 [32, 92160], P(None, 'lat')
The draws below stay inside these ranges and needn't reach their ends.
Inputs may be any that keep to these rules, and one draw needn't show every extreme that they name: `neighbours`: points are numbered row by row: latitude row i holds points i * 360 to (i + 1) * 360 - 1. Rows 0 and 1 name the east and west neighbour in the same latitude row (cyclic in longitude); rows 2 and 3 name a point of the latitude row before and after, at most one column away (cyclic); -1 where the grid has no such row.
All inputs are finite; a program needn't handle non-finite values.
Results may differ from the reference program's by a relative error of at most 0.0001.
Values sent between devices are 32-bit elements; how exact they have to be, the bound alone decides.
No kernel may reach another device: no remote copies, remote signals or barrier semaphores. Data moves between devices by JAX's collectives and lax.ppermute only.
A program may use at most 64 MiB of HBM per device.

```python
import jax
import jax.numpy as jnp
from jax import lax

VARS = 8
RANK = 32
NLON = 360
SWEEPS = 8
NLAT = 256
POINTS = 92160
HOURS = 256


def draw_neighbours(key, part):
    offsets = jax.random.randint(jax.random.fold_in(key, 17), (2, POINTS), -1, 2)
    positions = jnp.arange(POINTS, dtype=jnp.int32)
    row_index = positions // NLON
    column = positions % NLON
    east = row_index * NLON + (column + 1) % NLON
    west = row_index * NLON + (column - 1 + NLON) % NLON
    north = jnp.where(row_index > 0, (row_index - 1) * NLON + (column + offsets[0] + NLON) % NLON, -1)
    south = jnp.where(row_index < NLAT - 1, (row_index + 1) * NLON + (column + offsets[1] + NLON) % NLON, -1)
    return jnp.stack([east, west, north, south]).astype(jnp.int32)


def levels(rng, dims, pieces, least, high):
    def one(position, parts):
        draws = jax.random.uniform(jax.random.fold_in(jax.random.fold_in(rng, 6), position), (parts,), jnp.float32, least / len(pieces), high / len(pieces))
        return jnp.repeat(jnp.exp(draws), dims[position] // parts).reshape((-1,) + (1,) * (len(dims) - position - 1))

    gain = one(*pieces[0])
    for cut in pieces[1:]:
        gain = gain * one(*cut)
    return gain


def normal_values(rng, dims, spread, bound, pieces=(), kind=jnp.bfloat16):
    values = spread * jax.random.normal(rng, dims, jnp.float32)
    if pieces:
        values = values * levels(rng, dims, pieces, -0.22, 0.18)
    return jnp.clip(values, -bound, bound).astype(kind)


def setup_inputs(seed: int = 0) -> dict:
    keys = jax.random.split(jax.random.key(seed), 6)
    data = normal_values(keys[0], (VARS, HOURS, POINTS), 1.0, 6.0, ((1, 16), (2, 16)), jnp.float32)
    space_init = normal_values(keys[1], (RANK, POINTS), POINTS ** -0.5, 0.01953125, ((1, 16),), jnp.float32)
    time_init = normal_values(keys[2], (RANK, HOURS), 1.0, 6.0, ((1, 16),), jnp.float32)
    variable_factor = normal_values(keys[3], (VARS, RANK), VARS ** -0.5, 2.0, (), jnp.float32)
    neighbours = draw_neighbours(jax.random.fold_in(keys[5], 71), 0)
    return {"data": data, "space_init": space_init, "time_init": time_init, "variable_factor": variable_factor, "neighbours": neighbours}


def inverse(matrix):
    lower = jnp.linalg.cholesky(matrix)
    identity = jnp.eye(matrix.shape[0], dtype=jnp.float32)
    return jax.scipy.linalg.cho_solve((lower, True), identity)

def reference(data, space_init, time_init, variable_factor, neighbours):
    highest = lax.Precision.HIGHEST
    var_count, hour_count, point_count = data.shape
    rank_count = space_init.shape[0]
    identity = jnp.eye(rank_count, dtype=jnp.float32)
    unfolded = data.reshape(var_count * hour_count, point_count)
    var_gram = jnp.dot(variable_factor.T.astype(jnp.float32), variable_factor.astype(jnp.float32), precision=highest, preferred_element_type=jnp.float32)
    space_gram = lax.dot_general(space_init.astype(jnp.float32), space_init.astype(jnp.float32), (((1,), (1,)), ((), ())), precision=highest, preferred_element_type=jnp.float32)
    projected = lax.dot_general(space_init.astype(jnp.float32), unfolded.astype(jnp.float32), (((1,), (1,)), ((), ())), precision=highest, preferred_element_type=jnp.float32)
    projected = projected.reshape(rank_count, var_count, hour_count)
    time_rhs = lax.optimization_barrier(jnp.sum(projected * variable_factor.T[:, :, None], axis=1))
    padded = jnp.pad(time_init, ((0, 0), (2, 2)))
    stencil = padded[:, :-4] - 4.0 * padded[:, 1:-3] - 4.0 * padded[:, 3:-1] + padded[:, 4:]
    time_inv = inverse(space_gram * var_gram + 3.0 * identity)
    time_factor = jnp.dot(time_inv.astype(jnp.float32), (time_rhs - 0.5 * stencil).astype(jnp.float32), precision=highest, preferred_element_type=jnp.float32)
    time_gram = lax.dot_general(time_factor.astype(jnp.float32), time_factor.astype(jnp.float32), (((1,), (1,)), ((), ())), precision=highest, preferred_element_type=jnp.float32)
    scale = jnp.sqrt(jnp.diagonal(time_gram) + 1e-06)
    point_op = time_gram / (scale[:, None] * scale[None, :]) * var_gram + 2.0 * identity
    point_inv = inverse(point_op)
    weighted = (variable_factor.T[:, :, None] * time_factor[:, None, :]).reshape(rank_count, var_count * hour_count)
    point_rhs = jnp.dot(weighted.astype(jnp.float32), unfolded.astype(jnp.float32), precision=highest, preferred_element_type=jnp.float32) / scale[:, None]
    valid = neighbours >= 0
    clipped = jnp.maximum(neighbours, 0).reshape(-1)
    current = space_init
    for sweep_index in range(SWEEPS):
        near = jnp.take(current, clipped, axis=1).reshape(rank_count, 4, point_count)
        near_sum = lax.optimization_barrier(jnp.sum(jnp.where(valid[None], near, jnp.float32(0.0)), axis=1))
        current = jnp.dot(point_inv.astype(jnp.float32), (point_rhs + 0.5 * near_sum).astype(jnp.float32), precision=highest, preferred_element_type=jnp.float32)
    return (time_factor, current)
```

```python
import jax
import jax.numpy as jnp
from jax import lax
from jax.experimental import pallas as pl
from jax.experimental.pallas import tpu as pltpu
from jax.sharding import PartitionSpec as P

RANK = 32
NLON = 360
ROWS = 16
SWEEPS = 8
LANES = 128
PARTS = 4
WIDTH = NLON // PARTS
HIGHEST = lax.Precision.HIGHEST
F32 = jnp.float32
NT = (((1,), (1,)), ((), ()))

Y_GROUPS = [[y * 4 + z for y in range(4)] for z in range(4)]
Z_GROUPS = [[y * 4 + z for z in range(4)] for y in range(4)]
SWAP_NEAR = [(i, i ^ 1) for i in range(16)]
SWAP_FAR = [(i, (i + 1) % 16 if i % 2 else (i - 1) % 16) for i in range(16)]


def lane_iota(rows):
    return lax.broadcasted_iota(jnp.int32, (rows, LANES), 1)


def row_iota(rows):
    return lax.broadcasted_iota(jnp.int32, (rows, LANES), 0)


def turn(x, shift):
    shift = shift % LANES
    return x if shift == 0 else pltpu.roll(x, shift, axis=1)


def packed(rep, width):
    lane = lane_iota(8)
    total = jnp.zeros((8, LANES), F32)
    for g in range(4):
        here = (lane >= g * width) & (lane < (g + 1) * width)
        total = jnp.where(here, rep[8 * g : 8 * g + 8], total)
    return total


def unpacked(pack, width, at):
    lane = lane_iota(8)
    keep = (lane >= at) & (lane < at + width)
    tiles = [jnp.where(keep, turn(pack, at - g * width), 0.0) for g in range(4)]
    return jnp.concatenate(tiles, axis=0)


def eliminated(a):
    row = row_iota(RANK)
    for k in range(RANK):
        pivot_row = a[k : k + 1, :]
        q = pivot_row / pivot_row[:, k : k + 1]
        a = jnp.where(row == k, q, a - a[:, k : k + 1] * q)
    return a


def project_kernel(data_ref, space_ref, vf_ref, out_ref, proj_ref, gram_ref):
    step = pl.program_id(0)

    @pl.when(step == 0)
    def _():
        proj_ref[...] = jnp.zeros_like(proj_ref)
        gram_ref[...] = jnp.zeros_like(gram_ref)

    space = space_ref[...]
    data = data_ref[...].reshape(LANES, space.shape[1])
    proj_ref[...] += lax.dot_general(space, data, NT, precision=HIGHEST, preferred_element_type=F32)
    four = jnp.concatenate([space] * 4, axis=0)
    gram_ref[...] += lax.dot_general(space, four, NT, precision=HIGHEST, preferred_element_type=F32)

    @pl.when(step == pl.num_programs(0) - 1)
    def _():
        rhs = proj_ref[...] * vf_ref[...]
        for s in (64, 32, 16):
            rhs = rhs + turn(rhs, s)
        g = packed(gram_ref[...], 32)
        r = packed(rhs, 16)
        for k in range(16):
            out_ref[k, :, 0:128] = g
            out_ref[k, :, 128:256] = r


def project(data, space, vf_lanes):
    chunk = 1152
    return pl.pallas_call(
        project_kernel,
        grid=(5760 // chunk,),
        in_specs=[
            pl.BlockSpec((8, 16, chunk), lambda i: (0, 0, i)),
            pl.BlockSpec((RANK, chunk), lambda i: (0, i)),
            pl.BlockSpec((RANK, LANES), lambda i: (0, 0)),
        ],
        out_specs=pl.BlockSpec((16, 8, 256), lambda i: (0, 0, 0)),
        out_shape=jax.ShapeDtypeStruct((16, 8, 256), F32),
        scratch_shapes=[pltpu.VMEM((RANK, LANES), F32), pltpu.VMEM((RANK, LANES), F32)],
        name="project",
    )(data, space, vf_lanes)


def window(ref, start):
    count = ref.shape[1] // LANES
    t0, off = start // LANES, start % LANES
    lo = ref[:, t0 * LANES : (t0 + 1) * LANES] if 0 <= t0 < count else None
    t1 = t0 + 1
    hi = ref[:, t1 * LANES : (t1 + 1) * LANES] if off and 0 <= t1 < count else None
    if lo is None:
        return turn(hi, -off)
    if hi is None:
        return turn(lo, -off)
    lane = lane_iota(ref.shape[0])
    return jnp.where(lane < LANES - off, turn(lo, -off), turn(hi, -off))


def hour_kernel(got_ref, side_ref, vg_ref, vf_ref, data_ref, tf_ref, out_ref, dbuf, terms, sem):
    copy = pltpu.make_async_copy(data_ref, dbuf, sem)
    copy.start()
    total = got_ref[0]
    for k in range(1, 16):
        total = total + got_ref[k]
    lane = lane_iota(RANK)
    eye = jnp.where(lane == row_iota(RANK), 1.0, 0.0)
    gram = unpacked(total[:, 0:128], 32, 0)
    rhs = unpacked(total[:, 128:256], 16, 32)
    a = gram * vg_ref[...] + 3.0 * eye + rhs + side_ref[...]
    a = eliminated(a)
    tf = jnp.where((lane >= 32) & (lane < 48), a, 0.0)
    tf_ref[...] = turn(tf, -32)[:, 0:16]
    four = jnp.concatenate([tf] * 4, axis=0)
    hour_gram = packed(
        lax.dot_general(tf, four, NT, precision=HIGHEST, preferred_element_type=F32), 32
    )
    rep = tf
    for s in (64, 32, 16):
        rep = rep + turn(rep, s)
    weighted = rep * vf_ref[...]
    copy.wait()
    for c in range(5):
        at = slice(c * 1152, (c + 1) * 1152)
        terms[:, at] = jnp.dot(
            weighted,
            dbuf[:, :, at].reshape(LANES, 1152),
            precision=HIGHEST,
            preferred_element_type=F32,
        )
    for i in range(ROWS):
        base = i * NLON
        for y in range(PARTS):
            w = window(terms, base + y * WIDTH - 8)
            if y == 0:
                w = jnp.where(lane < 8, window(terms, base + NLON - 8), w)
            if y == PARTS - 1:
                w = jnp.where(lane < 98, w, window(terms, base - 98))
            for z in range(4):
                out_ref[y * 4 + z, :, i * LANES : (i + 1) * LANES] = w[8 * z : 8 * z + 8]
    for k in range(16):
        out_ref[k, :, ROWS * LANES :] = hour_gram


def hour_mode(got, side, vg_lanes, vf_lanes, data):
    vmem = pl.BlockSpec(memory_space=pltpu.VMEM)
    return pl.pallas_call(
        hour_kernel,
        in_specs=[vmem, vmem, vmem, vmem, pl.BlockSpec(memory_space=pl.ANY)],
        out_specs=(vmem, vmem),
        out_shape=(
            jax.ShapeDtypeStruct((RANK, 16), F32),
            jax.ShapeDtypeStruct((16, 8, ROWS * LANES + LANES), F32),
        ),
        scratch_shapes=[
            pltpu.VMEM((8, 16, 5760), F32),
            pltpu.VMEM((RANK, 5760), F32),
            pltpu.SemaphoreType.DMA,
        ],
        name="hour_mode",
    )(got, side, vg_lanes, vf_lanes, data)


def total_kernel(got_ref, piece_ref, gram_ref):
    for c in range(ROWS + 1):
        at = slice(c * LANES, (c + 1) * LANES)
        total = got_ref[0, :, at]
        for k in range(1, 16):
            total = total + got_ref[k, :, at]
        if c < ROWS:
            for k in range(4):
                piece_ref[k, :, at] = total
        else:
            gram_ref[...] = total


def totals(got):
    vmem = pl.BlockSpec(memory_space=pltpu.VMEM)
    return pl.pallas_call(
        total_kernel,
        in_specs=[vmem],
        out_specs=(vmem, vmem),
        out_shape=(
            jax.ShapeDtypeStruct((4, 8, ROWS * LANES), F32),
            jax.ShapeDtypeStruct((8, LANES), F32),
        ),
        name="totals",
    )(got)


def operator_kernel(gram_ref, vg_ref, weight_ref, scale_ref):
    lane = lane_iota(RANK)
    row = row_iota(RANK)
    on_diag = lane == row
    gram = unpacked(gram_ref[...], 32, 0)
    diag = jnp.where(on_diag, gram, 0.0)
    scale_col = jnp.sqrt(jnp.sum(diag, axis=1, keepdims=True) + 1e-06)
    scale_row = jnp.sqrt(jnp.sum(diag, axis=0, keepdims=True) + 1e-06)
    op = gram / (scale_col * scale_row) * vg_ref[...] + 2.0 * jnp.where(on_diag, 1.0, 0.0)
    a = eliminated(op + jnp.where(lane == row + 32, 1.0, 0.0))
    inv = jnp.where((lane >= 32) & (lane < 64), a, 0.0)
    high = inv.astype(jnp.bfloat16).astype(F32)
    low = inv - high
    weight = turn(high, -32) + high + turn(low, 32) + turn(low, 64)
    weight_ref[...] = weight.astype(jnp.bfloat16)
    scale_ref[...] = jnp.broadcast_to(scale_col, (RANK, LANES))


def operator(gram, vg_lanes):
    vmem = pl.BlockSpec(memory_space=pltpu.VMEM)
    return pl.pallas_call(
        operator_kernel,
        in_specs=[vmem, vmem],
        out_specs=(vmem, vmem),
        out_shape=(
            jax.ShapeDtypeStruct((RANK, LANES), jnp.bfloat16),
            jax.ShapeDtypeStruct((RANK, LANES), F32),
        ),
        name="operator",
        cost_estimate=pl.CostEstimate(flops=10_000_000, bytes_accessed=100_000, transcendentals=0),
    )(gram, vg_lanes)


EXT = ROWS + 16


def sweep_kernel(even_ref, rhs_ref, near_ref, far_ref, start_ref, weight_ref, scale_ref, out_ref, state, rhs, x4):
    even = even_ref[0] == 1
    scale = scale_ref[...]
    for i in range(1, EXT - 1):
        at = slice(i * LANES, (i + 1) * LANES)
        if i < 8:
            h = slice((i - 1) * LANES, i * LANES)
            v = jnp.where(even, far_ref[:, h], near_ref[:, h])
        elif i < 8 + ROWS:
            v = rhs_ref[:, (i - 8) * LANES : (i - 7) * LANES]
        else:
            h = slice((i - 24) * LANES, (i - 23) * LANES)
            v = jnp.where(even, near_ref[:, h], far_ref[:, h])
        rhs[:, at] = v / scale
    for i in range(EXT):
        at = slice(i * LANES, (i + 1) * LANES)
        state[:, at] = start_ref[0:RANK, at]
    weight = weight_ref[...]

    def line(i):
        c = state[:, i * LANES : (i + 1) * LANES]
        return (turn(c, -1), c, turn(c, 1))

    def pick(code, triple):
        ahead, same, behind = triple
        return jnp.where(
            code == 2.0,
            ahead,
            jnp.where(code == 3.0, behind, jnp.where(code == 1.0, same, 0.0)),
        )

    def sweep(_, carry):
        before, here = line(0), line(1)
        for i in range(1, EXT - 1):
            at = slice(i * LANES, (i + 1) * LANES)
            after = line(i + 1)
            north = jnp.broadcast_to(start_ref[RANK : RANK + 1, at], (RANK, LANES))
            south = jnp.broadcast_to(start_ref[RANK + 1 : RANK + 2, at], (RANK, LANES))
            near = here[0] + here[2] + pick(north, before) + pick(south, after)
            x = rhs[:, at] + 0.5 * near
            high = x.astype(jnp.bfloat16)
            low = (x - high.astype(F32)).astype(jnp.bfloat16)
            x4[0:32, at] = high
            x4[32:64, at] = low
            x4[64:96, at] = high
            x4[96:128, at] = low
            before, here = here, after
        for c in range(EXT // 2):
            first, last = max(1, 2 * c), min(EXT - 1, 2 * c + 2)
            at = slice(first * LANES, last * LANES)
            state[:, at] = jnp.dot(weight, x4[:, at], preferred_element_type=F32)
        return carry

    lax.fori_loop(0, SWEEPS, sweep, 0)
    lane = lane_iota(RANK)
    tiles = {}
    for i in range(ROWS):
        c = state[:, (8 + i) * LANES : (9 + i) * LANES]
        t, off = i * WIDTH // LANES, i * WIDTH % LANES
        moved = turn(c, off - 8)
        tiles[t] = jnp.where(lane < off, tiles[t], moved) if t in tiles else moved
        if off + WIDTH > LANES:
            tiles[t + 1] = moved
    for t in sorted(tiles):
        for k in range(PARTS):
            out_ref[k, :, t * LANES : (t + 1) * LANES] = tiles[t]


def sweeps(even, rhs, near, far, start, weight, scale):
    vmem = pl.BlockSpec(memory_space=pltpu.VMEM)
    return pl.pallas_call(
        sweep_kernel,
        in_specs=[pl.BlockSpec(memory_space=pltpu.SMEM)] + [vmem] * 6,
        out_specs=vmem,
        out_shape=jax.ShapeDtypeStruct((PARTS, RANK, 12 * LANES), F32),
        scratch_shapes=[
            pltpu.VMEM((RANK, EXT * LANES), F32),
            pltpu.VMEM((RANK, EXT * LANES), F32),
            pltpu.VMEM((4 * RANK, EXT * LANES), jnp.bfloat16),
        ],
        name="sweeps",
    )(even, rhs, near, far, start, weight, scale)


def join_kernel(got_ref, out_ref):
    lane = lane_iota(RANK)
    tiles = {}
    for i in range(ROWS):
        for y in range(PARTS):
            src, dst = i * WIDTH, i * NLON + y * WIDTH
            w = window(got_ref.at[y], src)
            t, off = dst // LANES, dst % LANES
            moved = turn(w, off)
            tiles[t] = jnp.where(lane < off, tiles[t], moved) if t in tiles else moved
            if off + WIDTH > LANES:
                tiles[t + 1] = moved
    for t in sorted(tiles):
        out_ref[:, t * LANES : (t + 1) * LANES] = tiles[t]


def join(got):
    vmem = pl.BlockSpec(memory_space=pltpu.VMEM)
    return pl.pallas_call(
        join_kernel,
        in_specs=[vmem],
        out_specs=vmem,
        out_shape=jax.ShapeDtypeStruct((RANK, ROWS * NLON), F32),
        name="join",
    )(got)


def link_codes(links):
    column = jnp.arange(links.shape[1], dtype=jnp.int32) % NLON
    target = (links % NLON - column + NLON) % NLON
    code = jnp.where(target == 1, 2.0, jnp.where(target == NLON - 1, 3.0, 1.0))
    return jnp.where(links >= 0, code, 0.0).astype(F32)


def swapped(edge_near, edge_far):
    return (
        lax.ppermute(edge_near, "lat", SWAP_NEAR),
        lax.ppermute(edge_far, "lat", SWAP_FAR),
    )


def edges(block, rows, even):
    width = rows * LANES
    top, bottom = block[:, :width], block[:, block.shape[1] - width :]
    return swapped(jnp.where(even, bottom, top), jnp.where(even, top, bottom))


def per_device(data, space_init, time_init, variable_factor, neighbours):
    tm = lax.axis_index("tm")
    lat = lax.axis_index("lat")
    even = lat % 2 == 0
    part = tm // 4
    vf_lanes = jnp.repeat(variable_factor.T, 16, axis=1)
    var_gram = jnp.dot(variable_factor.T, variable_factor, precision=HIGHEST, preferred_element_type=F32)
    vg_lanes = jnp.pad(var_gram, ((0, 0), (0, LANES - RANK)))

    sums = project(data, space_init, vf_lanes)
    got = lax.all_to_all(sums, "lat", 0, 0, tiled=True)

    low = lax.ppermute(time_init[:, -2:], "tm", [(i, (i + 1) % 16) for i in range(16)])
    high = lax.ppermute(time_init[:, :2], "tm", [((i + 1) % 16, i) for i in range(16)])
    low = jnp.where(tm == 0, 0.0, low)
    high = jnp.where(tm == 15, 0.0, high)
    padded = jnp.concatenate([low, time_init, high], axis=1)
    stencil = padded[:, :-4] - 4.0 * padded[:, 1:-3] - 4.0 * padded[:, 3:-1] + padded[:, 4:]
    side = jnp.pad(-0.5 * stencil, ((0, 0), (32, 80)))

    own = jnp.concatenate([space_init, link_codes(neighbours[2:4])], axis=0)
    own = own.reshape(RANK + 2, ROWS, NLON)
    own = jnp.concatenate([own[:, :, NLON - 8 :], own, own[:, :, :30]], axis=2)
    own = lax.dynamic_slice_in_dim(own, part * WIDTH, LANES, axis=2)
    own = own.reshape(RANK + 2, ROWS * LANES)
    start_near, start_far = edges(own, 8, even)
    start = jnp.concatenate(
        [
            jnp.where(even, start_far, start_near),
            own,
            jnp.where(even, start_near, start_far),
        ],
        axis=1,
    )

    time_factor, terms = hour_mode(got, side, vg_lanes, vf_lanes, data)
    got = lax.all_to_all(terms, "tm", 0, 0, tiled=True)
    pieces, gram = totals(got)
    rhs = lax.all_to_all(pieces, "tm", 0, 0, tiled=True, axis_index_groups=Z_GROUPS)
    weight, scale = operator(gram, vg_lanes)
    rhs = rhs.reshape(RANK, ROWS * LANES)
    near, far = edges(rhs, 7, even)
    even_flag = jnp.where(even, 1, 0).astype(jnp.int32).reshape(1)
    blocks = sweeps(even_flag, rhs, near, far, start, weight, scale)
    blocks = lax.all_to_all(blocks, "tm", 0, 0, tiled=True, axis_index_groups=Y_GROUPS)
    return (time_factor, join(blocks))


def solution(mesh):
    placed = (P(None, "tm", "lat"), P(None, "lat"), P(None, "tm"), P(), P(None, "lat"))
    return jax.shard_map(
        per_device,
        mesh=mesh,
        in_specs=placed,
        out_specs=(P(None, "tm"), P(None, "lat")),
        check_vma=False,
    )
```

```python
import jax
import jax.numpy as jnp
from jax import lax
from jax.experimental import pallas as pl
from jax.experimental.pallas import tpu as pltpu
from jax.sharding import PartitionSpec as P


RANK = 32
NLON = 360
ROWS = 16
SWEEPS = 8
LANES = 128
PARTS = 4
WIDTH = NLON // PARTS
STRIDE = WIDTH + 14
PIECE = ROWS * STRIDE
HIGHEST = lax.Precision.HIGHEST
F32 = jnp.float32
NT = (((1,), (1,)), ((), ()))

Y_GROUPS = [[y * 4 + z for y in range(4)] for z in range(4)]
Z_GROUPS = [[y * 4 + z for z in range(4)] for y in range(4)]
SWAP_NEAR = [(i, i ^ 1) for i in range(16)]
SWAP_FAR = [(i, (i + 1) % 16 if i % 2 else (i - 1) % 16) for i in range(16)]


def lane_iota(rows):
    return lax.broadcasted_iota(jnp.int32, (rows, LANES), 1)


def row_iota(rows):
    return lax.broadcasted_iota(jnp.int32, (rows, LANES), 0)


def turn(x, shift):
    shift = shift % LANES
    return x if shift == 0 else pltpu.roll(x, shift, axis=1)


def packed(rep, width):
    lane = lane_iota(8)
    total = jnp.zeros((8, LANES), F32)
    for g in range(4):
        here = (lane >= g * width) & (lane < (g + 1) * width)
        total = jnp.where(here, rep[8 * g : 8 * g + 8], total)
    return total


def unpacked(pack, width, at):
    lane = lane_iota(8)
    keep = (lane >= at) & (lane < at + width)
    tiles = [jnp.where(keep, turn(pack, at - g * width), 0.0) for g in range(4)]
    return jnp.concatenate(tiles, axis=0)


def eliminated(a):
    row = row_iota(RANK)
    for k in range(RANK):
        pivot_row = a[k : k + 1, :]
        q = pivot_row / pivot_row[:, k : k + 1]
        a = jnp.where(row == k, q, a - a[:, k : k + 1] * q)
    return a


def split_3(x):
    first = x.astype(jnp.bfloat16)
    rest = x - first.astype(F32)
    second = rest.astype(jnp.bfloat16)
    third = (rest - second.astype(F32)).astype(jnp.bfloat16)
    return first, second, third


def factor_lanes(vf):
    eye = jnp.where(lax.broadcasted_iota(jnp.int32, (RANK, RANK), 0) == lax.broadcasted_iota(jnp.int32, (RANK, RANK), 1), 1.0, 0.0)
    turned = lax.dot_general(eye, vf, NT, precision=HIGHEST, preferred_element_type=F32)
    chosen = jnp.where(lane_iota(8) // 16 == row_iota(8), 1.0, 0.0)
    return jnp.dot(turned, chosen, precision=HIGHEST, preferred_element_type=F32)


def project_kernel(data_ref, space_ref, vf_ref, out_ref, acc_ref):
    step = pl.program_id(0)

    @pl.when(step == 0)
    def _():
        acc_ref[...] = jnp.zeros_like(acc_ref)

    space = space_ref[...]
    data = data_ref[...].reshape(LANES, space.shape[1])
    d1, d2, d3 = split_3(data)
    s1, s2, s3 = split_3(space)
    x1 = jnp.concatenate([d1, s1], axis=0)
    x2 = jnp.concatenate([d2, s2], axis=0)
    x3 = jnp.concatenate([d3, s3], axis=0)
    p1 = lax.dot_general(jnp.concatenate([s1, s2, s3], axis=0), x1, NT, preferred_element_type=F32)
    p2 = lax.dot_general(jnp.concatenate([s1, s2], axis=0), x2, NT, preferred_element_type=F32)
    p3 = lax.dot_general(s1, x3, NT, preferred_element_type=F32)
    small = p1[64:96] + p2[32:64] + p3
    acc_ref[...] += p1[0:32] + (p1[32:64] + p2[0:32] + small)

    @pl.when(step == pl.num_programs(0) - 1)
    def _():
        rhs = acc_ref[:, 0:LANES] * factor_lanes(vf_ref[...])
        for s in (64, 32, 16):
            rhs = rhs + turn(rhs, s)
        gram = jnp.concatenate([acc_ref[:, LANES:]] * 4, axis=1)
        g = packed(gram, 32)
        r = packed(rhs, 16)
        for k in range(16):
            out_ref[k, :, 0:128] = g
            out_ref[k, :, 128:256] = r


def project(data, space, vf):
    chunk = 1152
    return pl.pallas_call(
        project_kernel,
        grid=(5760 // chunk,),
        in_specs=[
            pl.BlockSpec((8, 16, chunk), lambda i: (0, 0, i)),
            pl.BlockSpec((RANK, chunk), lambda i: (0, i)),
            pl.BlockSpec((8, RANK), lambda i: (0, 0)),
        ],
        out_specs=pl.BlockSpec((16, 8, 256), lambda i: (0, 0, 0)),
        out_shape=jax.ShapeDtypeStruct((16, 8, 256), F32),
        scratch_shapes=[pltpu.VMEM((RANK, LANES + RANK), F32)],
        cost_estimate=pl.CostEstimate(flops=4_000_000_000, bytes_accessed=8_000_000, transcendentals=0),
        name="project",
    )(data, space, vf)


def grant(mebibytes):
    return pltpu.CompilerParams(vmem_limit_bytes=mebibytes * 1024 * 1024)


def pack_pieces(pieces, width, store):
    lane = lane_iota(RANK)
    held = None
    for i, piece in enumerate(pieces):
        t, off = divmod(i * width, LANES)
        moved = turn(piece, off)
        value = moved if off == 0 else jnp.where(lane < off, held, moved)
        if off + width >= LANES:
            store(t, value)
            held = moved
        else:
            held = value
    if (i + 1) * width % LANES:
        store((i + 1) * width // LANES, held)


def spot(start):
    return lax.div(start, LANES), lax.rem(start, LANES)


def placed(ref, start, to):
    t, off = divmod(start, LANES)
    lo, hi = ref[:, t * LANES : (t + 1) * LANES], ref[:, (t + 1) * LANES : (t + 2) * LANES]
    return turn(jnp.where(lane_iota(RANK) >= off, lo, hi), to - off)


def window(ref, start):
    count = ref.shape[1] // LANES
    t0, off = start // LANES, start % LANES
    lo = ref[:, t0 * LANES : (t0 + 1) * LANES] if 0 <= t0 < count else None
    t1 = t0 + 1
    hi = ref[:, t1 * LANES : (t1 + 1) * LANES] if off and 0 <= t1 < count else None
    if lo is None:
        return turn(hi, -off)
    if hi is None:
        return turn(lo, -off)
    return turn(jnp.where(lane_iota(ref.shape[0]) >= off, lo, hi), -off)


def tile(t):
    return pl.ds(pl.multiple_of(t * LANES, LANES), LANES)


def hour_kernel(got_ref, side_ref, vg_ref, vf_ref, data_ref, tf_ref, out_ref, dbuf, terms, sem):
    copy = pltpu.make_async_copy(data_ref, dbuf, sem)
    copy.start()
    total = got_ref[0]
    for k in range(1, 16):
        total = total + got_ref[k]
    lane = lane_iota(RANK)
    eye = jnp.where(lane == row_iota(RANK), 1.0, 0.0)
    gram = unpacked(total[:, 0:128], 32, 0)
    rhs = unpacked(total[:, 128:256], 16, 32)
    a = gram * vg_ref[...] + 3.0 * eye + rhs + side_ref[...]
    a = eliminated(a)
    tf = jnp.where((lane >= 32) & (lane < 48), a, 0.0)
    tf_ref[...] = turn(tf, -32)[:, 0:16]
    four = jnp.concatenate([tf] * 4, axis=0)
    hour_gram = packed(
        lax.dot_general(tf, four, NT, precision=HIGHEST, preferred_element_type=F32), 32
    )
    rep = tf
    for s in (64, 32, 16):
        rep = rep + turn(rep, s)
    weighted = rep * factor_lanes(vf_ref[...])
    copy.wait()
    w1, w2, w3 = split_3(weighted)
    w123 = jnp.concatenate([w1, w2, w3], axis=0)
    for c in range(5):
        at = slice(c * 1152, (c + 1) * 1152)
        d1, d2, d3 = split_3(dbuf[:, :, at].reshape(LANES, 1152))
        p1 = jnp.dot(w123, d1, preferred_element_type=F32)
        p2 = jnp.dot(w123[0:64], d2, preferred_element_type=F32)
        p3 = jnp.dot(w1, d3, preferred_element_type=F32)
        terms[:, at] = p1[0:32] + (p1[32:64] + p2[0:32] + (p1[64:96] + p2[32:64] + p3))
    for y in range(PARTS):

        def store(t, value):
            for z in range(4):
                out_ref[y * 4 + z, :, t * LANES : (t + 1) * LANES] = value[8 * z : 8 * z + 8]

        held = None
        for i in range(ROWS):
            t, off = divmod(i * STRIDE, LANES)
            base = i * NLON
            spin = lax.rem(lane + LANES - off, LANES)
            if y == 0:
                moved = placed(terms, base, off + 7)
                moved = jnp.where(spin < 7, placed(terms, base + NLON - 7, off), moved)
            else:
                moved = placed(terms, base + y * WIDTH - 7, off)
            if y == PARTS - 1:
                moved = jnp.where(spin < 97, moved, placed(terms, base, off + 97))
            value = moved if off == 0 else jnp.where(lane < off, held, moved)
            held = value
            if off + STRIDE >= LANES:
                store(t, value)
                held = moved
    for k in range(16):
        out_ref[k, :, PIECE:] = hour_gram


def hour_mode(got, side, vg_lanes, vf, data):
    vmem = pl.BlockSpec(memory_space=pltpu.VMEM)
    return pl.pallas_call(
        hour_kernel,
        in_specs=[vmem, vmem, vmem, vmem, pl.BlockSpec(memory_space=pl.ANY)],
        out_specs=(vmem, vmem),
        out_shape=(
            jax.ShapeDtypeStruct((RANK, 16), F32),
            jax.ShapeDtypeStruct((16, 8, PIECE + LANES), F32),
        ),
        scratch_shapes=[
            pltpu.VMEM((8, 16, 5760), F32),
            pltpu.VMEM((RANK, 5760 + LANES), F32),
            pltpu.SemaphoreType.DMA,
        ],
        compiler_params=grant(62),
        cost_estimate=pl.CostEstimate(flops=5_000_000_000, bytes_accessed=8_000_000, transcendentals=0),
        name="hour_mode",
    )(got, side, vg_lanes, vf, data)


def total_kernel(got_ref, piece_ref, gram_ref):
    for c in range(PIECE // LANES + 1):
        at = slice(c * LANES, (c + 1) * LANES)
        total = got_ref[0, :, at]
        for k in range(1, 16):
            total = total + got_ref[k, :, at]
        if c < PIECE // LANES:
            for k in range(4):
                piece_ref[k, :, at] = total
        else:
            gram_ref[...] = total


def totals(got):
    vmem = pl.BlockSpec(memory_space=pltpu.VMEM)
    return pl.pallas_call(
        total_kernel,
        in_specs=[vmem],
        out_specs=(vmem, vmem),
        out_shape=(
            jax.ShapeDtypeStruct((4, 8, PIECE), F32),
            jax.ShapeDtypeStruct((8, LANES), F32),
        ),
        compiler_params=grant(8),
        name="totals",
    )(got)


def operator_kernel(gram_ref, vg_ref, weight_ref, inv_ref, scale_ref):
    lane = lane_iota(RANK)
    row = row_iota(RANK)
    on_diag = lane == row
    gram = unpacked(gram_ref[...], 32, 0)
    diag = jnp.where(on_diag, gram, 0.0)
    scale_col = jnp.sqrt(jnp.sum(diag, axis=1, keepdims=True) + 1e-06)
    scale_row = jnp.sqrt(jnp.sum(diag, axis=0, keepdims=True) + 1e-06)
    op = gram / (scale_col * scale_row) * vg_ref[...] + 2.0 * jnp.where(on_diag, 1.0, 0.0)
    a = eliminated(op + jnp.where(lane == row + 32, 1.0, 0.0))
    inv = jnp.where((lane >= 32) & (lane < 64), a, 0.0)
    half = 0.5 * inv
    high = half.astype(jnp.bfloat16).astype(F32)
    low = half - high
    weight = turn(high, -32) + high + turn(low, 32) + turn(low, 64)
    weight_ref[...] = weight.astype(jnp.bfloat16)
    inv_ref[...] = turn(inv, -32)
    scale_ref[...] = jnp.broadcast_to(scale_col, (RANK, LANES))


def operator(gram, vg_lanes):
    vmem = pl.BlockSpec(memory_space=pltpu.VMEM)
    return pl.pallas_call(
        operator_kernel,
        in_specs=[vmem, vmem],
        out_specs=(vmem, vmem, vmem),
        out_shape=(
            jax.ShapeDtypeStruct((RANK, LANES), jnp.bfloat16),
            jax.ShapeDtypeStruct((RANK, LANES), F32),
            jax.ShapeDtypeStruct((RANK, LANES), F32),
        ),
        name="operator",
        compiler_params=grant(4),
        cost_estimate=pl.CostEstimate(flops=4_000_000_000, bytes_accessed=100_000, transcendentals=0),
    )(gram, vg_lanes)


EXT = ROWS + 16
EDGE = 6 * LANES


def sweep_kernel(
    even_ref, rhs_ref, near_ref, far_ref, start_ref, weight_ref, inv_ref, scale_ref, out_ref, state, base, x4, codes
):
    even = even_ref[0] == 1
    scale = scale_ref[...]
    inv = inv_ref[:, 0:RANK]
    for i in range(1, EXT - 1):
        at = slice(i * LANES, (i + 1) * LANES)
        if i < 8:
            first = (i + 8) * STRIDE - (PIECE - EDGE) - 1
            v = jnp.where(even, window(far_ref, first), window(near_ref, first))
        elif i < 8 + ROWS:
            v = window(rhs_ref, (i - 8) * STRIDE - 1)
        else:
            first = (i - 24) * STRIDE - 1
            v = jnp.where(even, window(near_ref, first), window(far_ref, first))
        state[:, at] = v / scale
    for c in range(EXT // 2):
        at = slice(max(1, 2 * c) * LANES, min(EXT - 1, 2 * c + 2) * LANES)
        base[:, at] = jnp.dot(inv, state[:, at], precision=HIGHEST, preferred_element_type=F32)
    for i in range(EXT):
        at = slice(i * LANES, (i + 1) * LANES)
        state[:, at] = start_ref[0:RANK, at]
        codes[0:8, at] = jnp.broadcast_to(start_ref[RANK : RANK + 1, at], (8, LANES))
        codes[8:16, at] = jnp.broadcast_to(start_ref[RANK + 1 : RANK + 2, at], (8, LANES))
    weight = weight_ref[...]

    def line(i):
        at = slice(i * LANES, (i + 1) * LANES)
        tiles = [state[8 * g : 8 * g + 8, at] for g in range(4)]
        return [(turn(c, -1), c, turn(c, 1)) for c in tiles]

    def sweep(_, carry):
        before, here = line(0), line(1)
        for i in range(1, EXT - 1):
            at = slice(i * LANES, (i + 1) * LANES)
            after = line(i + 1)
            picks = [[codes[8 * d : 8 * d + 8, at] == k for k in (1.0, 2.0, 3.0)] for d in range(2)]

            def pick(d, triple):
                ahead, same, behind = triple
                same_at, ahead_at, behind_at = picks[d]
                rest = jnp.where(same_at, same, 0.0)
                return jnp.where(ahead_at, ahead, jnp.where(behind_at, behind, rest))

            near = jnp.concatenate(
                [
                    (here[g][0] + here[g][2]) + (pick(0, before[g]) + pick(1, after[g]))
                    for g in range(4)
                ],
                axis=0,
            )
            high = near.astype(jnp.bfloat16)
            low = (near - high.astype(F32)).astype(jnp.bfloat16)
            x4[0:32, at] = high
            x4[32:64, at] = low
            x4[64:96, at] = high
            x4[96:128, at] = low
            before, here = here, after
        for c in range(EXT // 2):
            first, last = max(1, 2 * c), min(EXT - 1, 2 * c + 2)
            at = slice(first * LANES, last * LANES)
            state[:, at] = base[:, at] + jnp.dot(weight, x4[:, at], preferred_element_type=F32)
        return carry

    lax.fori_loop(0, SWEEPS, sweep, 0)

    def store(t, value):
        for k in range(PARTS):
            out_ref[k, :, t * LANES : (t + 1) * LANES] = value

    pack_pieces(
        [turn(state[:, (8 + i) * LANES : (9 + i) * LANES], -8) for i in range(ROWS)], WIDTH, store
    )


def sweeps(even, rhs, near, far, start, weight, inv, scale):
    vmem = pl.BlockSpec(memory_space=pltpu.VMEM)
    return pl.pallas_call(
        sweep_kernel,
        in_specs=[pl.BlockSpec(memory_space=pltpu.SMEM)] + [vmem] * 7,
        out_specs=vmem,
        out_shape=jax.ShapeDtypeStruct((PARTS, RANK, 12 * LANES), F32),
        scratch_shapes=[
            pltpu.VMEM((RANK, EXT * LANES), F32),
            pltpu.VMEM((RANK, EXT * LANES), F32),
            pltpu.VMEM((4 * RANK, EXT * LANES), jnp.bfloat16),
            pltpu.VMEM((16, EXT * LANES), F32),
        ],
        compiler_params=grant(12),
        name="sweeps",
    )(even, rhs, near, far, start, weight, inv, scale)


def join_kernel(got_ref, out_ref):
    lane = lane_iota(RANK)

    def row(i, held):
        for y in range(PARTS):
            to_tile, off = spot(i * NLON + y * WIDTH)
            first, at = spot(i * WIDTH)
            joint = jnp.where(lane >= at, got_ref[y, :, tile(first)], got_ref[y, :, tile(first + 1)])
            moved = pltpu.roll(joint, lax.rem(off + LANES - at, LANES), axis=1)
            value = jnp.where(lane < off, held, moved)
            out_ref[:, tile(to_tile)] = value
            held = jnp.where(off + WIDTH >= LANES, moved, value)
        return held

    lax.fori_loop(0, ROWS, row, jnp.zeros((RANK, LANES), F32))


def join(got):
    vmem = pl.BlockSpec(memory_space=pltpu.VMEM)
    return pl.pallas_call(
        join_kernel,
        in_specs=[vmem],
        out_specs=vmem,
        out_shape=jax.ShapeDtypeStruct((RANK, ROWS * NLON), F32),
        compiler_params=grant(8),
        name="join",
    )(got)


def link_codes(links):
    column = jnp.arange(links.shape[1], dtype=jnp.int32) % NLON
    target = (links % NLON - column + NLON) % NLON
    code = jnp.where(target == 1, 2.0, jnp.where(target == NLON - 1, 3.0, 1.0))
    return jnp.where(links >= 0, code, 0.0).astype(F32)


def swapped(edge_near, edge_far):
    far = lax.ppermute(edge_far, "lat", SWAP_FAR)
    near = lax.ppermute(edge_near, "lat", SWAP_NEAR)
    return near, far


def edges(block, width, even):
    top, bottom = block[:, :width], block[:, block.shape[1] - width :]
    return swapped(jnp.where(even, bottom, top), jnp.where(even, top, bottom))


def per_device(data, space_init, time_init, variable_factor, neighbours):
    tm = lax.axis_index("tm")
    lat = lax.axis_index("lat")
    even = lat % 2 == 0
    part = tm // 4

    hours = time_init.T
    low = lax.ppermute(hours[-2:], "tm", [(i, (i + 1) % 16) for i in range(16)])
    high = lax.ppermute(hours[:2], "tm", [((i + 1) % 16, i) for i in range(16)])
    sums = project(data, space_init, variable_factor)
    got = lax.all_to_all(sums, "lat", 0, 0, tiled=True)

    var_gram = jnp.dot(variable_factor.T, variable_factor, precision=HIGHEST, preferred_element_type=F32)
    vg_lanes = jnp.pad(var_gram, ((0, 0), (0, LANES - RANK)))
    low = jnp.where(tm == 0, 0.0, low)
    high = jnp.where(tm == 15, 0.0, high)
    padded = jnp.concatenate([low, hours, high], axis=0)
    stencil = padded[:-4] - 4.0 * padded[1:-3] - 4.0 * padded[3:-1] + padded[4:]
    side = jnp.pad((-0.5 * stencil).T, ((0, 0), (32, 80)))

    own = jnp.concatenate([space_init, link_codes(neighbours[2:4])], axis=0)
    own, _ = lax.optimization_barrier((own, sums[0, 0, 0]))
    own = own.reshape(RANK + 2, ROWS, NLON)
    own = jnp.concatenate([own[:, :, NLON - 8 :], own, own[:, :, :30]], axis=2)
    own = lax.dynamic_slice_in_dim(own, part * WIDTH, LANES, axis=2)
    own = own.reshape(RANK + 2, ROWS * LANES)
    start_near, start_far = edges(own, 8 * LANES, even)
    start = jnp.concatenate(
        [
            jnp.where(even, start_far, start_near),
            own,
            jnp.where(even, start_near, start_far),
        ],
        axis=1,
    )

    time_factor, terms = hour_mode(got, side, vg_lanes, variable_factor, data)
    got = lax.all_to_all(terms, "tm", 0, 0, tiled=True)
    pieces, gram = totals(got)
    rhs = lax.all_to_all(pieces, "tm", 0, 0, tiled=True, axis_index_groups=Z_GROUPS)
    weight, inv, scale = operator(gram, vg_lanes)
    rhs = rhs.reshape(RANK, PIECE)
    near, far = edges(rhs, EDGE, even)
    even_flag = jnp.where(even, 1, 0).astype(jnp.int32).reshape(1)
    blocks = sweeps(even_flag, rhs, near, far, start, weight, inv, scale)
    blocks = lax.all_to_all(blocks, "tm", 0, 0, tiled=True, axis_index_groups=Y_GROUPS)
    return (time_factor, join(blocks))


def solution(mesh):
    placed_at = (P(None, "tm", "lat"), P(None, "lat"), P(None, "tm"), P(), P(None, "lat"))
    return jax.shard_map(
        per_device,
        mesh=mesh,
        in_specs=placed_at,
        out_specs=(P(None, "tm"), P(None, "lat")),
        check_vma=False,
    )
```

```python
import jax
import jax.numpy as jnp
from jax import lax
from jax.experimental import pallas as pl
from jax.experimental.pallas import tpu as pltpu
from jax.sharding import PartitionSpec as P


RANK = 32
NLON = 360
ROWS = 16
SWEEPS = 8
LANES = 128
PARTS = 4
WIDTH = NLON // PARTS
STRIDE = WIDTH + 14
PIECE = ROWS * STRIDE
HIGHEST = lax.Precision.HIGHEST
F32 = jnp.float32
NT = (((1,), (1,)), ((), ()))

Y_GROUPS = [[y * 4 + z for y in range(4)] for z in range(4)]
Z_GROUPS = [[y * 4 + z for z in range(4)] for y in range(4)]
SWAP_NEAR = [(i, i ^ 1) for i in range(16)]
SWAP_FAR = [(i, (i + 1) % 16 if i % 2 else (i - 1) % 16) for i in range(16)]


def lane_iota(rows):
    return lax.broadcasted_iota(jnp.int32, (rows, LANES), 1)


def row_iota(rows):
    return lax.broadcasted_iota(jnp.int32, (rows, LANES), 0)


def turn(x, shift):
    shift = shift % LANES
    return x if shift == 0 else pltpu.roll(x, shift, axis=1)


def packed(rep, width):
    lane = lane_iota(8)
    total = jnp.zeros((8, LANES), F32)
    for g in range(4):
        here = (lane >= g * width) & (lane < (g + 1) * width)
        total = jnp.where(here, rep[8 * g : 8 * g + 8], total)
    return total


def unpacked(pack, width, at):
    lane = lane_iota(8)
    keep = (lane >= at) & (lane < at + width)
    tiles = [jnp.where(keep, turn(pack, at - g * width), 0.0) for g in range(4)]
    return jnp.concatenate(tiles, axis=0)


def eliminated(a):
    row = row_iota(RANK)
    for k in range(RANK):
        pivot_row = a[k : k + 1, :]
        q = pivot_row / pivot_row[:, k : k + 1]
        a = jnp.where(row == k, q, a - a[:, k : k + 1] * q)
    return a


def split_3(x):
    first = x.astype(jnp.bfloat16)
    rest = x - first.astype(F32)
    second = rest.astype(jnp.bfloat16)
    third = (rest - second.astype(F32)).astype(jnp.bfloat16)
    return first, second, third


def factor_lanes(vf):
    eye = jnp.where(lax.broadcasted_iota(jnp.int32, (RANK, RANK), 0) == lax.broadcasted_iota(jnp.int32, (RANK, RANK), 1), 1.0, 0.0)
    turned = lax.dot_general(eye, vf, NT, precision=HIGHEST, preferred_element_type=F32)
    chosen = jnp.where(lane_iota(8) // 16 == row_iota(8), 1.0, 0.0)
    return jnp.dot(turned, chosen, precision=HIGHEST, preferred_element_type=F32)


TN = (((0,), (0,)), ((), ()))


def gram_lanes(vf):
    chosen = jnp.where(lane_iota(RANK) == row_iota(RANK), 1.0, 0.0)
    wide = jnp.dot(vf, chosen, precision=HIGHEST, preferred_element_type=F32)
    return lax.dot_general(vf, wide, TN, precision=HIGHEST, preferred_element_type=F32)


def project_kernel(data_ref, space_ref, vf_ref, out_ref, acc_ref):
    step = pl.program_id(0)

    @pl.when(step == 0)
    def _():
        acc_ref[...] = jnp.zeros_like(acc_ref)

    space = space_ref[...]
    data = data_ref[...].reshape(LANES, space.shape[1])
    d1, d2, d3 = split_3(data)
    s1, s2, s3 = split_3(space)
    x1 = jnp.concatenate([d1, s1], axis=0)
    x2 = jnp.concatenate([d2, s2], axis=0)
    x3 = jnp.concatenate([d3, s3], axis=0)
    side = jnp.concatenate([s1, s2, s3, s1], axis=0)
    first, mid, last = acc_ref.at[0], acc_ref.at[1], acc_ref.at[2]
    first[...] += lax.dot_general(x1, side, NT, preferred_element_type=F32)
    mid[...] += lax.dot_general(x2, side, NT, preferred_element_type=F32)
    last[...] += lax.dot_general(x3, side, NT, preferred_element_type=F32)

    @pl.when(step == pl.num_programs(0) - 1)
    def _():
        p1, p2, p3 = acc_ref[0], acc_ref[1], acc_ref[2]
        total = p1 + (turn(p1, -32) + p2 + (turn(p1, -64) + turn(p2, -32) + p3))
        rhs = jnp.transpose(total[0:LANES])[0:RANK] * factor_lanes(vf_ref[...])
        for s in (64, 32, 16):
            rhs = rhs + turn(rhs, s)
        gram = jnp.where(lane_iota(RANK) < RANK, total[LANES:], 0.0)
        gram = gram + turn(gram, 32)
        gram = gram + turn(gram, 64)
        g = packed(gram, 32)
        r = packed(rhs, 16)
        for k in range(16):
            out_ref[k, :, 0:128] = g
            out_ref[k, :, 128:256] = r


def project(data, space, vf):
    chunk = 5760
    return pl.pallas_call(
        project_kernel,
        grid=(5760 // chunk,),
        in_specs=[
            pl.BlockSpec((8, 16, chunk), lambda i: (0, 0, i)),
            pl.BlockSpec((RANK, chunk), lambda i: (0, i)),
            pl.BlockSpec((8, RANK), lambda i: (0, 0)),
        ],
        out_specs=pl.BlockSpec((16, 8, 256), lambda i: (0, 0, 0)),
        out_shape=jax.ShapeDtypeStruct((16, 8, 256), F32),
        scratch_shapes=[pltpu.VMEM((3, LANES + RANK, LANES), F32)],
        cost_estimate=pl.CostEstimate(flops=4_000_000_000, bytes_accessed=8_000_000, transcendentals=0),
        name="project",
    )(data, space, vf)


def grant(mebibytes):
    return pltpu.CompilerParams(vmem_limit_bytes=int(mebibytes * 1024 * 1024))


def pack_pieces(pieces, width, store):
    lane = lane_iota(RANK)
    held = None
    for i, piece in enumerate(pieces):
        t, off = divmod(i * width, LANES)
        moved = turn(piece, off)
        value = moved if off == 0 else jnp.where(lane < off, held, moved)
        if off + width >= LANES:
            store(t, value)
            held = moved
        else:
            held = value
    if (i + 1) * width % LANES:
        store((i + 1) * width // LANES, held)


def spot(start):
    return lax.div(start, LANES), lax.rem(start, LANES)


def placed(ref, start, to):
    t, off = divmod(start, LANES)
    lo, hi = ref[:, t * LANES : (t + 1) * LANES], ref[:, (t + 1) * LANES : (t + 2) * LANES]
    return turn(jnp.where(lane_iota(RANK) >= off, lo, hi), to - off)


def window(ref, start):
    count = ref.shape[1] // LANES
    t0, off = start // LANES, start % LANES
    lo = ref[:, t0 * LANES : (t0 + 1) * LANES] if 0 <= t0 < count else None
    t1 = t0 + 1
    hi = ref[:, t1 * LANES : (t1 + 1) * LANES] if off and 0 <= t1 < count else None
    if lo is None:
        return turn(hi, -off)
    if hi is None:
        return turn(lo, -off)
    return turn(jnp.where(lane_iota(ref.shape[0]) >= off, lo, hi), -off)


def tile(t):
    return pl.ds(pl.multiple_of(t * LANES, LANES), LANES)


def hour_kernel(got_ref, stencil_ref, vf_ref, data_ref, tf_ref, out_ref, dbuf, terms, sem):
    copy = pltpu.make_async_copy(data_ref, dbuf, sem)
    copy.start()
    total = got_ref[0]
    for k in range(1, 16):
        total = total + got_ref[k]
    lane = lane_iota(RANK)
    eye = jnp.where(lane == row_iota(RANK), 1.0, 0.0)
    gram = unpacked(total[:, 0:128], 32, 0)
    rhs = unpacked(total[:, 128:256], 16, 32)
    vf = vf_ref[...]
    chosen = jnp.where(lane_iota(16) == row_iota(16) + 32, 1.0, 0.0)
    stencil = lax.dot_general(
        stencil_ref[...], chosen, TN, precision=HIGHEST, preferred_element_type=F32
    )
    a = gram * gram_lanes(vf) + 3.0 * eye + rhs - 0.5 * stencil
    a = eliminated(a)
    tf = jnp.where((lane >= 32) & (lane < 48), a, 0.0)
    tf_ref[...] = turn(tf, -32)[:, 0:16]
    four = jnp.concatenate([tf] * 4, axis=0)
    hour_gram = packed(
        lax.dot_general(tf, four, NT, precision=HIGHEST, preferred_element_type=F32), 32
    )
    rep = tf
    for s in (64, 32, 16):
        rep = rep + turn(rep, s)
    weighted = rep * factor_lanes(vf)
    copy.wait()
    w1, w2, w3 = split_3(weighted)
    w123 = jnp.concatenate([w1, w2, w3], axis=0)
    for c in range(5):
        at = slice(c * 1152, (c + 1) * 1152)
        d1, d2, d3 = split_3(dbuf[:, :, at].reshape(LANES, 1152))
        p1 = jnp.dot(w123, d1, preferred_element_type=F32)
        p2 = jnp.dot(w123[0:64], d2, preferred_element_type=F32)
        p3 = jnp.dot(w1, d3, preferred_element_type=F32)
        terms[:, at] = p1[0:32] + (p1[32:64] + p2[0:32] + (p1[64:96] + p2[32:64] + p3))
    for y in range(PARTS):

        def store(t, value):
            out_ref[y, :, t * LANES : (t + 1) * LANES] = value

        held = None
        for i in range(ROWS):
            t, off = divmod(i * STRIDE, LANES)
            base = i * NLON
            spin = lax.rem(lane + LANES - off, LANES)
            if y == 0:
                moved = placed(terms, base, off + 7)
                moved = jnp.where(spin < 7, placed(terms, base + NLON - 7, off), moved)
            else:
                moved = placed(terms, base + y * WIDTH - 7, off)
            if y == PARTS - 1:
                moved = jnp.where(spin < 97, moved, placed(terms, base, off + 97))
            value = moved if off == 0 else jnp.where(lane < off, held, moved)
            held = value
            if off + STRIDE >= LANES:
                store(t, value)
                held = moved
    for y in range(PARTS):
        out_ref[y, :, PIECE:] = jnp.concatenate([hour_gram] * 4, axis=0)


def hour_mode(got, stencil, vf, data):
    vmem = pl.BlockSpec(memory_space=pltpu.VMEM)
    return pl.pallas_call(
        hour_kernel,
        in_specs=[vmem, vmem, vmem, pl.BlockSpec(memory_space=pl.ANY)],
        out_specs=(vmem, vmem),
        out_shape=(
            jax.ShapeDtypeStruct((RANK, 16), F32),
            jax.ShapeDtypeStruct((PARTS, RANK, PIECE + LANES), F32),
        ),
        scratch_shapes=[
            pltpu.VMEM((8, 16, 5760), F32),
            pltpu.VMEM((RANK, 5760 + LANES), F32),
            pltpu.SemaphoreType.DMA,
        ],
        compiler_params=grant(61.5),
        cost_estimate=pl.CostEstimate(flops=5_000_000_000, bytes_accessed=8_000_000, transcendentals=0),
        name="hour_mode",
    )(got, stencil, vf, data)


def total_kernel(got_ref, piece_ref, gram_ref):
    for c in range(PIECE // LANES + 1):
        at = slice(c * LANES, (c + 1) * LANES)
        total = got_ref[0, :, at]
        for k in range(1, 4):
            total = total + got_ref[k, :, at]
        if c < PIECE // LANES:
            for k in range(4):
                piece_ref[k, :, at] = total
        else:
            gram_ref[...] = total


def part_kernel(got_ref, out_ref):
    for z in range(4):
        for c in range(PIECE // LANES + 1):
            at = slice(c * LANES, (c + 1) * LANES)
            rows = slice(8 * z, 8 * z + 8)
            a, b = got_ref[0, rows, at] + got_ref[1, rows, at], got_ref[2, rows, at] + got_ref[3, rows, at]
            out_ref[z, :, at] = a + b


def part_totals(got):
    vmem = pl.BlockSpec(memory_space=pltpu.VMEM)
    return pl.pallas_call(
        part_kernel,
        in_specs=[vmem],
        out_specs=vmem,
        out_shape=jax.ShapeDtypeStruct((4, 8, PIECE + LANES), F32),
        compiler_params=grant(8),
        name="part_totals",
    )(got)


def totals(got):
    vmem = pl.BlockSpec(memory_space=pltpu.VMEM)
    return pl.pallas_call(
        total_kernel,
        in_specs=[vmem],
        out_specs=(vmem, vmem),
        out_shape=(
            jax.ShapeDtypeStruct((4, 8, PIECE), F32),
            jax.ShapeDtypeStruct((8, LANES), F32),
        ),
        compiler_params=grant(8),
        name="totals",
    )(got)


def operator_kernel(gram_ref, vf_ref, weight_ref, inv_ref, scale_ref):
    lane = lane_iota(RANK)
    row = row_iota(RANK)
    on_diag = lane == row
    gram = unpacked(gram_ref[...], 32, 0)
    diag = jnp.where(on_diag, gram, 0.0)
    scale_col = jnp.sqrt(jnp.sum(diag, axis=1, keepdims=True) + 1e-06)
    scale_row = jnp.sqrt(jnp.sum(diag, axis=0, keepdims=True) + 1e-06)
    op = gram / (scale_col * scale_row) * gram_lanes(vf_ref[...]) + 2.0 * jnp.where(on_diag, 1.0, 0.0)
    a = eliminated(op + jnp.where(lane == row + 32, 1.0, 0.0))
    inv = jnp.where((lane >= 32) & (lane < 64), a, 0.0)
    half = 0.5 * inv
    high = half.astype(jnp.bfloat16).astype(F32)
    low = half - high
    weight = turn(high, -32) + high + turn(low, 32) + turn(low, 64)
    weight_ref[...] = weight.astype(jnp.bfloat16)
    i1, i2, i3 = (part.astype(F32) for part in split_3(inv))
    inv_ref[:, 0:128] = (turn(i1, -32) + i1 + turn(i1, 32) + turn(i2, 64)).astype(jnp.bfloat16)
    inv_ref[:, 128:256] = (turn(i2, -32) + i3).astype(jnp.bfloat16)
    scale_ref[...] = jnp.broadcast_to(scale_col, (RANK, LANES))


def operator(gram, vf):
    vmem = pl.BlockSpec(memory_space=pltpu.VMEM)
    return pl.pallas_call(
        operator_kernel,
        in_specs=[vmem, vmem],
        out_specs=(vmem, vmem, vmem),
        out_shape=(
            jax.ShapeDtypeStruct((RANK, LANES), jnp.bfloat16),
            jax.ShapeDtypeStruct((RANK, 2 * LANES), jnp.bfloat16),
            jax.ShapeDtypeStruct((RANK, LANES), F32),
        ),
        name="operator",
        compiler_params=grant(4),
        cost_estimate=pl.CostEstimate(flops=4_000_000_000, bytes_accessed=100_000, transcendentals=0),
    )(gram, vf)


EXT = ROWS + 16
EDGE = 6 * LANES


def sweep_kernel(
    even_ref, rhs_ref, near_ref, far_ref, start_ref, weight_ref, inv_ref, scale_ref, out_ref, state, base, codes
):
    even = even_ref[0] == 1
    scale = scale_ref[...]
    inv = inv_ref[:, 0 : 6 * RANK]
    for i in range(1, EXT - 1):
        at = slice(i * LANES, (i + 1) * LANES)
        if i < 8:
            first = (i + 8) * STRIDE - (PIECE - EDGE) - 1
            v = jnp.where(even, window(far_ref, first), window(near_ref, first))
        elif i < 8 + ROWS:
            v = window(rhs_ref, (i - 8) * STRIDE - 1)
        else:
            first = (i - 24) * STRIDE - 1
            v = jnp.where(even, window(near_ref, first), window(far_ref, first))
        state[:, at] = v / scale
    for c in range(EXT // 2):
        at = slice(max(1, 2 * c) * LANES, min(EXT - 1, 2 * c + 2) * LANES)
        x1, x2, x3 = split_3(state[:, at])
        x6 = jnp.concatenate([x1, x2, x3, x1, x2, x1], axis=0)
        base[:, at] = jnp.dot(inv, x6, preferred_element_type=F32)
    for i in range(EXT):
        at = slice(i * LANES, (i + 1) * LANES)
        state[:, at] = start_ref[0:RANK, at]
        codes[0:8, at] = jnp.broadcast_to(start_ref[RANK : RANK + 1, at], (8, LANES))
        codes[8:16, at] = jnp.broadcast_to(start_ref[RANK + 1 : RANK + 2, at], (8, LANES))
    weight = weight_ref[...]

    def line(i):
        at = slice(i * LANES, (i + 1) * LANES)
        tiles = [state[8 * g : 8 * g + 8, at] for g in range(4)]
        return [(turn(c, -1), c, turn(c, 1)) for c in tiles]

    def sweep(_, carry):
        before, here = line(0), line(1)
        for i in range(1, EXT - 1):
            at = slice(i * LANES, (i + 1) * LANES)
            after = line(i + 1)
            picks = [[codes[8 * d : 8 * d + 8, at] == k for k in (1.0, 2.0, 3.0)] for d in range(2)]

            def pick(d, triple):
                ahead, same, behind = triple
                same_at, ahead_at, behind_at = picks[d]
                rest = jnp.where(same_at, same, 0.0)
                return jnp.where(ahead_at, ahead, jnp.where(behind_at, behind, rest))

            near = jnp.concatenate(
                [
                    (here[g][0] + here[g][2]) + (pick(0, before[g]) + pick(1, after[g]))
                    for g in range(4)
                ],
                axis=0,
            )
            pair = near if i % 2 == 0 or i == 1 else jnp.concatenate([pair, near], axis=1)
            if i % 2 == 1 or i == EXT - 2:
                last = (i + 1) * LANES
                done = slice(last - pair.shape[1], last)
                high = pair.astype(jnp.bfloat16)
                low = (pair - high.astype(F32)).astype(jnp.bfloat16)
                x4 = jnp.concatenate([high, low, high, low], axis=0)
                state[:, done] = base[:, done] + jnp.dot(weight, x4, preferred_element_type=F32)
            before, here = here, after
        return carry

    lax.fori_loop(0, SWEEPS, sweep, 0)

    def store(t, value):
        for k in range(PARTS):
            out_ref[k, :, t * LANES : (t + 1) * LANES] = value

    pack_pieces(
        [turn(state[:, (8 + i) * LANES : (9 + i) * LANES], -8) for i in range(ROWS)], WIDTH, store
    )


def sweeps(even, rhs, near, far, start, weight, inv, scale):
    vmem = pl.BlockSpec(memory_space=pltpu.VMEM)
    return pl.pallas_call(
        sweep_kernel,
        in_specs=[pl.BlockSpec(memory_space=pltpu.SMEM)] + [vmem] * 7,
        out_specs=vmem,
        out_shape=jax.ShapeDtypeStruct((PARTS, RANK, 12 * LANES), F32),
        scratch_shapes=[
            pltpu.VMEM((RANK, EXT * LANES), F32),
            pltpu.VMEM((RANK, EXT * LANES), F32),
            pltpu.VMEM((16, EXT * LANES), F32),
        ],
        compiler_params=grant(12),
        name="sweeps",
    )(even, rhs, near, far, start, weight, inv, scale)


def join_kernel(got_ref, out_ref):
    lane = lane_iota(RANK)

    def row(i, held):
        for y in range(PARTS):
            to_tile, off = spot(i * NLON + y * WIDTH)
            first, at = spot(i * WIDTH)
            joint = jnp.where(lane >= at, got_ref[y, :, tile(first)], got_ref[y, :, tile(first + 1)])
            moved = pltpu.roll(joint, lax.rem(off + LANES - at, LANES), axis=1)
            value = jnp.where(lane < off, held, moved)
            out_ref[:, tile(to_tile)] = value
            held = jnp.where(off + WIDTH >= LANES, moved, value)
        return held

    lax.fori_loop(0, ROWS, row, jnp.zeros((RANK, LANES), F32))


def join(got):
    vmem = pl.BlockSpec(memory_space=pltpu.VMEM)
    return pl.pallas_call(
        join_kernel,
        in_specs=[vmem],
        out_specs=vmem,
        out_shape=jax.ShapeDtypeStruct((RANK, ROWS * NLON), F32),
        compiler_params=grant(8),
        name="join",
    )(got)


def link_codes(links):
    column = jnp.arange(links.shape[1], dtype=jnp.int32) % NLON
    target = (links % NLON - column + NLON) % NLON
    code = jnp.where(target == 1, 2.0, jnp.where(target == NLON - 1, 3.0, 1.0))
    return jnp.where(links >= 0, code, 0.0).astype(F32)


def swapped(edge_near, edge_far):
    far = lax.ppermute(edge_far, "lat", SWAP_FAR)
    near = lax.ppermute(edge_near, "lat", SWAP_NEAR)
    return near, far


def chosen_edges(block, width, even):
    top, bottom = block[:, :width], block[:, block.shape[1] - width :]
    return jnp.where(even, bottom, top), jnp.where(even, top, bottom)


def per_device(data, space_init, time_init, variable_factor, neighbours):
    tm = lax.axis_index("tm")
    lat = lax.axis_index("lat")
    even = lat % 2 == 0
    part = tm // 4

    hours = time_init.T
    low = lax.ppermute(hours, "tm", [(i, (i + 1) % 16) for i in range(16)])
    high = lax.ppermute(hours, "tm", [((i + 1) % 16, i) for i in range(16)])
    sums = project(data, space_init, variable_factor)
    got = lax.all_to_all(sums, "lat", 0, 0, tiled=True)

    low = jnp.where(tm == 0, 0.0, low[-2:])
    high = jnp.where(tm == 15, 0.0, high[:2])
    padded = jnp.concatenate([low, hours, high], axis=0)
    stencil = padded[:-4] - 4.0 * padded[1:-3] - 4.0 * padded[3:-1] + padded[4:]

    own = jnp.concatenate([space_init, link_codes(neighbours[2:4])], axis=0)
    own, _ = lax.optimization_barrier((own, sums[0, 0, 0]))
    own = own.reshape(RANK + 2, ROWS, NLON)
    own = jnp.concatenate([own[:, :, NLON - 8 :], own, own[:, :, :30]], axis=2)
    own = lax.dynamic_slice_in_dim(own, part * WIDTH, LANES, axis=2)
    own = own.reshape(RANK + 2, ROWS * LANES)
    to_near, to_far = chosen_edges(own, 8 * LANES, even)
    to_near, to_far, got = lax.optimization_barrier((to_near, to_far, got))
    start_near, start_far = swapped(to_near, to_far)
    start = jnp.concatenate(
        [
            jnp.where(even, start_far, start_near),
            own,
            jnp.where(even, start_near, start_far),
        ],
        axis=1,
    )

    time_factor, terms = hour_mode(got, stencil, variable_factor, data)
    got = lax.all_to_all(terms, "tm", 0, 0, tiled=True, axis_index_groups=Y_GROUPS)
    got = lax.all_to_all(part_totals(got), "tm", 0, 0, tiled=True, axis_index_groups=Z_GROUPS)
    pieces, gram = totals(got)
    rhs = lax.all_to_all(pieces, "tm", 0, 0, tiled=True, axis_index_groups=Z_GROUPS)
    weight, inv, scale = operator(gram, variable_factor)
    rhs = rhs.reshape(RANK, PIECE)
    near, far = swapped(*chosen_edges(rhs, EDGE, even))
    even_flag = jnp.where(even, 1, 0).astype(jnp.int32).reshape(1)
    blocks = sweeps(even_flag, rhs, near, far, start, weight, inv, scale)
    blocks = lax.all_to_all(blocks, "tm", 0, 0, tiled=True, axis_index_groups=Y_GROUPS)
    return (time_factor, join(blocks))


def solution(mesh):
    placed_at = (P(None, "tm", "lat"), P(None, "lat"), P(None, "tm"), P(), P(None, "lat"))
    return jax.shard_map(
        per_device,
        mesh=mesh,
        in_specs=placed_at,
        out_specs=(P(None, "tm"), P(None, "lat")),
        check_vma=False,
    )
```

```python
import jax
import jax.numpy as jnp
from jax import lax
from jax.experimental import pallas as pl
from jax.experimental.pallas import tpu as pltpu
from jax.sharding import PartitionSpec as P


RANK = 32
NLON = 360
ROWS = 16
SWEEPS = 8
LANES = 128
PARTS = 4
WIDTH = NLON // PARTS
STRIDE = WIDTH + 14
PIECE = ROWS * STRIDE
HIGHEST = lax.Precision.HIGHEST
F32 = jnp.float32
NT = (((1,), (1,)), ((), ()))

Y_GROUPS = [[y * 4 + z for y in range(4)] for z in range(4)]
Z_GROUPS = [[y * 4 + z for z in range(4)] for y in range(4)]
SWAP_NEAR = [(i, i ^ 1) for i in range(16)]
SWAP_FAR = [(i, (i + 1) % 16 if i % 2 else (i - 1) % 16) for i in range(16)]


def lane_iota(rows):
    return lax.broadcasted_iota(jnp.int32, (rows, LANES), 1)


def row_iota(rows):
    return lax.broadcasted_iota(jnp.int32, (rows, LANES), 0)


def turn(x, shift):
    shift = shift % LANES
    return x if shift == 0 else pltpu.roll(x, shift, axis=1)


def packed(rep, width):
    lane = lane_iota(8)
    total = jnp.zeros((8, LANES), F32)
    for g in range(4):
        here = (lane >= g * width) & (lane < (g + 1) * width)
        total = jnp.where(here, rep[8 * g : 8 * g + 8], total)
    return total


def unpacked(pack, width, at):
    lane = lane_iota(8)
    keep = (lane >= at) & (lane < at + width)
    tiles = [jnp.where(keep, turn(pack, at - g * width), 0.0) for g in range(4)]
    return jnp.concatenate(tiles, axis=0)


def eliminated(a):
    row = row_iota(RANK)
    for k in range(RANK):
        pivot_row = a[k : k + 1, :]
        q = pivot_row / pivot_row[:, k : k + 1]
        a = jnp.where(row == k, q, a - a[:, k : k + 1] * q)
    return a


def split_3(x):
    first = x.astype(jnp.bfloat16)
    rest = x - first.astype(F32)
    second = rest.astype(jnp.bfloat16)
    third = (rest - second.astype(F32)).astype(jnp.bfloat16)
    return first, second, third


def factor_lanes(vf):
    eye = jnp.where(lax.broadcasted_iota(jnp.int32, (RANK, RANK), 0) == lax.broadcasted_iota(jnp.int32, (RANK, RANK), 1), 1.0, 0.0)
    turned = lax.dot_general(eye, vf, NT, precision=HIGHEST, preferred_element_type=F32)
    chosen = jnp.where(lane_iota(8) // 16 == row_iota(8), 1.0, 0.0)
    return jnp.dot(turned, chosen, precision=HIGHEST, preferred_element_type=F32)


TN = (((0,), (0,)), ((), ()))


def gram_lanes(vf):
    chosen = jnp.where(lane_iota(RANK) == row_iota(RANK), 1.0, 0.0)
    wide = jnp.dot(vf, chosen, precision=HIGHEST, preferred_element_type=F32)
    return lax.dot_general(vf, wide, TN, precision=HIGHEST, preferred_element_type=F32)


def project_kernel(data_ref, space_ref, vf_ref, out_ref, acc_ref):
    step = pl.program_id(0)

    @pl.when(step == 0)
    def _():
        acc_ref[...] = jnp.zeros_like(acc_ref)

    space = space_ref[...]
    data = data_ref[...].reshape(LANES, space.shape[1])
    d1, d2, d3 = split_3(data)
    s1, s2, s3 = split_3(space)
    x1 = jnp.concatenate([d1, s1], axis=0)
    x2 = jnp.concatenate([d2, s2], axis=0)
    x3 = jnp.concatenate([d3, s3], axis=0)
    side = jnp.concatenate([s1, s2, s3, s1], axis=0)
    first, mid, last = acc_ref.at[0], acc_ref.at[1], acc_ref.at[2]
    first[...] += lax.dot_general(x1, side, NT, preferred_element_type=F32)
    mid[...] += lax.dot_general(x2, side, NT, preferred_element_type=F32)
    last[...] += lax.dot_general(x3, side, NT, preferred_element_type=F32)

    @pl.when(step == pl.num_programs(0) - 1)
    def _():
        p1, p2, p3 = acc_ref[0], acc_ref[1], acc_ref[2]
        total = p1 + (turn(p1, -32) + p2 + (turn(p1, -64) + turn(p2, -32) + p3))
        rhs = jnp.transpose(total[0:LANES])[0:RANK] * factor_lanes(vf_ref[...])
        for s in (64, 32, 16):
            rhs = rhs + turn(rhs, s)
        gram = jnp.where(lane_iota(RANK) < RANK, total[LANES:], 0.0)
        gram = gram + turn(gram, 32)
        gram = gram + turn(gram, 64)
        g = packed(gram, 32)
        r = packed(rhs, 16)
        for k in range(16):
            out_ref[k, :, 0:128] = g
            out_ref[k, :, 128:256] = r


def project(data, space, vf):
    chunk = 5760
    return pl.pallas_call(
        project_kernel,
        grid=(5760 // chunk,),
        in_specs=[
            pl.BlockSpec((8, 16, chunk), lambda i: (0, 0, i)),
            pl.BlockSpec((RANK, chunk), lambda i: (0, i)),
            pl.BlockSpec((8, RANK), lambda i: (0, 0)),
        ],
        out_specs=pl.BlockSpec((16, 8, 256), lambda i: (0, 0, 0)),
        out_shape=jax.ShapeDtypeStruct((16, 8, 256), F32),
        scratch_shapes=[pltpu.VMEM((3, LANES + RANK, LANES), F32)],
        cost_estimate=pl.CostEstimate(flops=4_000_000_000, bytes_accessed=8_000_000, transcendentals=0),
        name="project",
    )(data, space, vf)


def grant(mebibytes):
    return pltpu.CompilerParams(vmem_limit_bytes=int(mebibytes * 1024 * 1024))


def pack_pieces(pieces, width, store):
    lane = lane_iota(RANK)
    held = None
    for i, piece in enumerate(pieces):
        t, off = divmod(i * width, LANES)
        moved = turn(piece, off)
        value = moved if off == 0 else jnp.where(lane < off, held, moved)
        if off + width >= LANES:
            store(t, value)
            held = moved
        else:
            held = value
    if (i + 1) * width % LANES:
        store((i + 1) * width // LANES, held)


def spot(start):
    return lax.div(start, LANES), lax.rem(start, LANES)


def placed(ref, start, to):
    t, off = divmod(start, LANES)
    lo, hi = ref[:, t * LANES : (t + 1) * LANES], ref[:, (t + 1) * LANES : (t + 2) * LANES]
    return turn(jnp.where(lane_iota(RANK) >= off, lo, hi), to - off)


def window(ref, start):
    count = ref.shape[1] // LANES
    t0, off = start // LANES, start % LANES
    lo = ref[:, t0 * LANES : (t0 + 1) * LANES] if 0 <= t0 < count else None
    t1 = t0 + 1
    hi = ref[:, t1 * LANES : (t1 + 1) * LANES] if off and 0 <= t1 < count else None
    if lo is None:
        return turn(hi, -off)
    if hi is None:
        return turn(lo, -off)
    return turn(jnp.where(lane_iota(ref.shape[0]) >= off, lo, hi), -off)


def tile(t):
    return pl.ds(pl.multiple_of(t * LANES, LANES), LANES)


def hour_kernel(got_ref, stencil_ref, vf_ref, data_ref, tf_ref, out_ref, dbuf, terms, sem):
    copy = pltpu.make_async_copy(data_ref, dbuf, sem)
    copy.start()
    total = got_ref[0]
    for k in range(1, 16):
        total = total + got_ref[k]
    lane = lane_iota(RANK)
    eye = jnp.where(lane == row_iota(RANK), 1.0, 0.0)
    gram = unpacked(total[:, 0:128], 32, 0)
    rhs = unpacked(total[:, 128:256], 16, 32)
    vf = vf_ref[...]
    chosen = jnp.where(lane_iota(16) == row_iota(16) + 32, 1.0, 0.0)
    stencil = lax.dot_general(
        stencil_ref[...], chosen, TN, precision=HIGHEST, preferred_element_type=F32
    )
    a = gram * gram_lanes(vf) + 3.0 * eye + rhs - 0.5 * stencil
    a = eliminated(a)
    tf = jnp.where((lane >= 32) & (lane < 48), a, 0.0)
    tf_ref[...] = turn(tf, -32)[:, 0:16]
    four = jnp.concatenate([tf] * 4, axis=0)
    hour_gram = packed(
        lax.dot_general(tf, four, NT, precision=HIGHEST, preferred_element_type=F32), 32
    )
    rep = tf
    for s in (64, 32, 16):
        rep = rep + turn(rep, s)
    weighted = rep * factor_lanes(vf)
    copy.wait()
    w1, w2, w3 = split_3(weighted)
    w123 = jnp.concatenate([w1, w2, w3], axis=0)
    for c in range(5):
        at = slice(c * 1152, (c + 1) * 1152)
        d1, d2, d3 = split_3(dbuf[:, :, at].reshape(LANES, 1152))
        p1 = jnp.dot(w123, d1, preferred_element_type=F32)
        p2 = jnp.dot(w123[0:64], d2, preferred_element_type=F32)
        p3 = jnp.dot(w1, d3, preferred_element_type=F32)
        terms[:, at] = p1[0:32] + (p1[32:64] + p2[0:32] + (p1[64:96] + p2[32:64] + p3))
    for y in range(PARTS):

        def store(t, value):
            out_ref[y, :, t * LANES : (t + 1) * LANES] = value

        held = None
        for i in range(ROWS):
            t, off = divmod(i * STRIDE, LANES)
            base = i * NLON
            spin = lax.rem(lane + LANES - off, LANES)
            if y == 0:
                moved = placed(terms, base, off + 7)
                moved = jnp.where(spin < 7, placed(terms, base + NLON - 7, off), moved)
            else:
                moved = placed(terms, base + y * WIDTH - 7, off)
            if y == PARTS - 1:
                moved = jnp.where(spin < 97, moved, placed(terms, base, off + 97))
            value = moved if off == 0 else jnp.where(lane < off, held, moved)
            held = value
            if off + STRIDE >= LANES:
                store(t, value)
                held = moved
    for y in range(PARTS):
        out_ref[y, :, PIECE:] = jnp.concatenate([hour_gram] * 4, axis=0)


def hour_mode(got, stencil, vf, data):
    vmem = pl.BlockSpec(memory_space=pltpu.VMEM)
    return pl.pallas_call(
        hour_kernel,
        in_specs=[vmem, vmem, vmem, pl.BlockSpec(memory_space=pl.ANY)],
        out_specs=(vmem, vmem),
        out_shape=(
            jax.ShapeDtypeStruct((RANK, 16), F32),
            jax.ShapeDtypeStruct((PARTS, RANK, PIECE + LANES), F32),
        ),
        scratch_shapes=[
            pltpu.VMEM((8, 16, 5760), F32),
            pltpu.VMEM((RANK, 5760 + LANES), F32),
            pltpu.SemaphoreType.DMA,
        ],
        compiler_params=grant(61.5),
        cost_estimate=pl.CostEstimate(flops=5_000_000_000, bytes_accessed=8_000_000, transcendentals=0),
        name="hour_mode",
    )(got, stencil, vf, data)


def total_kernel(got_ref, piece_ref, gram_ref):
    for c in range(PIECE // LANES + 1):
        at = slice(c * LANES, (c + 1) * LANES)
        total = got_ref[0, :, at]
        for k in range(1, 4):
            total = total + got_ref[k, :, at]
        if c < PIECE // LANES:
            for k in range(4):
                piece_ref[k, :, at] = total
        else:
            gram_ref[...] = total


def part_kernel(got_ref, out_ref):
    for z in range(4):
        for c in range(PIECE // LANES + 1):
            at = slice(c * LANES, (c + 1) * LANES)
            rows = slice(8 * z, 8 * z + 8)
            a, b = got_ref[0, rows, at] + got_ref[1, rows, at], got_ref[2, rows, at] + got_ref[3, rows, at]
            out_ref[z, :, at] = a + b


def part_totals(got):
    vmem = pl.BlockSpec(memory_space=pltpu.VMEM)
    return pl.pallas_call(
        part_kernel,
        in_specs=[vmem],
        out_specs=vmem,
        out_shape=jax.ShapeDtypeStruct((4, 8, PIECE + LANES), F32),
        compiler_params=grant(8),
        name="part_totals",
    )(got)


def totals(got):
    vmem = pl.BlockSpec(memory_space=pltpu.VMEM)
    return pl.pallas_call(
        total_kernel,
        in_specs=[vmem],
        out_specs=(vmem, vmem),
        out_shape=(
            jax.ShapeDtypeStruct((4, 8, PIECE), F32),
            jax.ShapeDtypeStruct((8, LANES), F32),
        ),
        compiler_params=grant(8),
        name="totals",
    )(got)


def operator_kernel(gram_ref, vf_ref, weight_ref, inv_ref, scale_ref):
    lane = lane_iota(RANK)
    row = row_iota(RANK)
    on_diag = lane == row
    gram = unpacked(gram_ref[...], 32, 0)
    diag = jnp.where(on_diag, gram, 0.0)
    scale_col = jnp.sqrt(jnp.sum(diag, axis=1, keepdims=True) + 1e-06)
    scale_row = jnp.sqrt(jnp.sum(diag, axis=0, keepdims=True) + 1e-06)
    op = gram / (scale_col * scale_row) * gram_lanes(vf_ref[...]) + 2.0 * jnp.where(on_diag, 1.0, 0.0)
    a = eliminated(op + jnp.where(lane == row + 32, 1.0, 0.0))
    inv = jnp.where((lane >= 32) & (lane < 64), a, 0.0)
    half = 0.5 * inv
    high = half.astype(jnp.bfloat16).astype(F32)
    low = half - high
    weight = turn(high, -32) + high + turn(low, 32) + turn(low, 64)
    weight_ref[...] = weight.astype(jnp.bfloat16)
    i1, i2, i3 = (part.astype(F32) for part in split_3(inv))
    inv_ref[:, 0:128] = (turn(i1, -32) + i1 + turn(i1, 32) + turn(i2, 64)).astype(jnp.bfloat16)
    inv_ref[:, 128:256] = (turn(i2, -32) + i3).astype(jnp.bfloat16)
    scale_ref[...] = jnp.broadcast_to(scale_col, (RANK, LANES))


def operator(gram, vf):
    vmem = pl.BlockSpec(memory_space=pltpu.VMEM)
    return pl.pallas_call(
        operator_kernel,
        in_specs=[vmem, vmem],
        out_specs=(vmem, vmem, vmem),
        out_shape=(
            jax.ShapeDtypeStruct((RANK, LANES), jnp.bfloat16),
            jax.ShapeDtypeStruct((RANK, 2 * LANES), jnp.bfloat16),
            jax.ShapeDtypeStruct((RANK, LANES), F32),
        ),
        name="operator",
        compiler_params=grant(4),
        cost_estimate=pl.CostEstimate(flops=4_000_000_000, bytes_accessed=100_000, transcendentals=0),
    )(gram, vf)


EXT = ROWS + 16
EDGE = 6 * LANES


def sweep_kernel(
    even_ref, rhs_ref, near_ref, far_ref, start_ref, weight_ref, inv_ref, scale_ref, out_ref, state, base, codes
):
    even = even_ref[0] == 1
    scale = scale_ref[...]
    inv = inv_ref[:, 0 : 6 * RANK]
    for i in range(1, EXT - 1):
        at = slice(i * LANES, (i + 1) * LANES)
        if i < 8:
            first = (i + 8) * STRIDE - (PIECE - EDGE) - 1
            v = jnp.where(even, window(far_ref, first), window(near_ref, first))
        elif i < 8 + ROWS:
            v = window(rhs_ref, (i - 8) * STRIDE - 1)
        else:
            first = (i - 24) * STRIDE - 1
            v = jnp.where(even, window(near_ref, first), window(far_ref, first))
        state[:, at] = v / scale
    for c in range(EXT // 2):
        at = slice(max(1, 2 * c) * LANES, min(EXT - 1, 2 * c + 2) * LANES)
        x1, x2, x3 = split_3(state[:, at])
        x6 = jnp.concatenate([x1, x2, x3, x1, x2, x1], axis=0)
        base[:, at] = jnp.dot(inv, x6, preferred_element_type=F32)
    for i in range(EXT):
        at = slice(i * LANES, (i + 1) * LANES)
        state[:, at] = start_ref[0:RANK, at]
        codes[0:8, at] = jnp.broadcast_to(start_ref[RANK : RANK + 1, at], (8, LANES))
        codes[8:16, at] = jnp.broadcast_to(start_ref[RANK + 1 : RANK + 2, at], (8, LANES))
    weight = weight_ref[...]

    def line(i):
        at = slice(i * LANES, (i + 1) * LANES)
        tiles = [state[8 * g : 8 * g + 8, at] for g in range(4)]
        return [(turn(c, -1), c, turn(c, 1)) for c in tiles]

    for step in range(SWEEPS):
        low_row, high_row = 1 + step, EXT - 1 - step
        before, here = line(low_row - 1), line(low_row)
        for i in range(low_row, high_row):
            at = slice(i * LANES, (i + 1) * LANES)
            after = line(i + 1)
            picks = [[codes[8 * d : 8 * d + 8, at] == k for k in (1.0, 2.0, 3.0)] for d in range(2)]

            def pick(d, triple):
                ahead, same, behind = triple
                same_at, ahead_at, behind_at = picks[d]
                rest = jnp.where(same_at, same, 0.0)
                return jnp.where(ahead_at, ahead, jnp.where(behind_at, behind, rest))

            near = jnp.concatenate(
                [
                    (here[g][0] + here[g][2]) + (pick(0, before[g]) + pick(1, after[g]))
                    for g in range(4)
                ],
                axis=0,
            )
            if (i - low_row) % 2 == 0:
                first = near
            else:
                pair = jnp.concatenate([first, near], axis=1)
                last = (i + 1) * LANES
                done = slice(last - pair.shape[1], last)
                high = pair.astype(jnp.bfloat16)
                low = (pair - high.astype(F32)).astype(jnp.bfloat16)
                x4 = jnp.concatenate([high, low, high, low], axis=0)
                state[:, done] = base[:, done] + jnp.dot(weight, x4, preferred_element_type=F32)
            before, here = here, after

    def store(t, value):
        for k in range(PARTS):
            out_ref[k, :, t * LANES : (t + 1) * LANES] = value

    pack_pieces(
        [turn(state[:, (8 + i) * LANES : (9 + i) * LANES], -8) for i in range(ROWS)], WIDTH, store
    )


def sweeps(even, rhs, near, far, start, weight, inv, scale):
    vmem = pl.BlockSpec(memory_space=pltpu.VMEM)
    return pl.pallas_call(
        sweep_kernel,
        in_specs=[pl.BlockSpec(memory_space=pltpu.SMEM)] + [vmem] * 7,
        out_specs=vmem,
        out_shape=jax.ShapeDtypeStruct((PARTS, RANK, 12 * LANES), F32),
        scratch_shapes=[
            pltpu.VMEM((RANK, EXT * LANES), F32),
            pltpu.VMEM((RANK, EXT * LANES), F32),
            pltpu.VMEM((16, EXT * LANES), F32),
        ],
        compiler_params=grant(12),
        name="sweeps",
    )(even, rhs, near, far, start, weight, inv, scale)


def join_kernel(got_ref, out_ref):
    lane = lane_iota(RANK)

    def row(i, held):
        for y in range(PARTS):
            to_tile, off = spot(i * NLON + y * WIDTH)
            first, at = spot(i * WIDTH)
            joint = jnp.where(lane >= at, got_ref[y, :, tile(first)], got_ref[y, :, tile(first + 1)])
            moved = pltpu.roll(joint, lax.rem(off + LANES - at, LANES), axis=1)
            value = jnp.where(lane < off, held, moved)
            out_ref[:, tile(to_tile)] = value
            held = jnp.where(off + WIDTH >= LANES, moved, value)
        return held

    lax.fori_loop(0, ROWS, row, jnp.zeros((RANK, LANES), F32), unroll=16)


def join(got):
    vmem = pl.BlockSpec(memory_space=pltpu.VMEM)
    return pl.pallas_call(
        join_kernel,
        in_specs=[vmem],
        out_specs=vmem,
        out_shape=jax.ShapeDtypeStruct((RANK, ROWS * NLON), F32),
        compiler_params=grant(8),
        name="join",
    )(got)


def link_codes(links):
    column = jnp.arange(links.shape[1], dtype=jnp.int32) % NLON
    target = (links % NLON - column + NLON) % NLON
    code = jnp.where(target == 1, 2.0, jnp.where(target == NLON - 1, 3.0, 1.0))
    return jnp.where(links >= 0, code, 0.0).astype(F32)


def swapped(edge_near, edge_far):
    far = lax.ppermute(edge_far, "lat", SWAP_FAR)
    near = lax.ppermute(edge_near, "lat", SWAP_NEAR)
    return near, far


def chosen_edges(block, width, even):
    top, bottom = block[:, :width], block[:, block.shape[1] - width :]
    return jnp.where(even, bottom, top), jnp.where(even, top, bottom)


def per_device(data, space_init, time_init, variable_factor, neighbours):
    tm = lax.axis_index("tm")
    lat = lax.axis_index("lat")
    even = lat % 2 == 0
    part = tm // 4

    hours = time_init.T
    low = lax.ppermute(hours, "tm", [(i, (i + 1) % 16) for i in range(16)])
    high = lax.ppermute(hours, "tm", [((i + 1) % 16, i) for i in range(16)])
    sums = project(data, space_init, variable_factor)
    got = lax.all_to_all(sums, "lat", 0, 0, tiled=True)

    low = jnp.where(tm == 0, 0.0, low[-2:])
    high = jnp.where(tm == 15, 0.0, high[:2])
    padded = jnp.concatenate([low, hours, high], axis=0)
    stencil = padded[:-4] - 4.0 * padded[1:-3] - 4.0 * padded[3:-1] + padded[4:]

    own = jnp.concatenate([space_init, link_codes(neighbours[2:4])], axis=0)
    own, _ = lax.optimization_barrier((own, sums[0, 0, 0]))
    own = own.reshape(RANK + 2, ROWS, NLON)
    own = jnp.concatenate([own[:, :, NLON - 8 :], own, own[:, :, :30]], axis=2)
    own = lax.dynamic_slice_in_dim(own, part * WIDTH, LANES, axis=2)
    own = own.reshape(RANK + 2, ROWS * LANES)
    to_near, to_far = chosen_edges(own, 8 * LANES, even)
    to_near, to_far, got = lax.optimization_barrier((to_near, to_far, got))
    start_near, start_far = swapped(to_near, to_far)
    start = jnp.concatenate(
        [
            jnp.where(even, start_far, start_near),
            own,
            jnp.where(even, start_near, start_far),
        ],
        axis=1,
    )

    time_factor, terms = hour_mode(got, stencil, variable_factor, data)
    got = lax.all_to_all(terms, "tm", 0, 0, tiled=True, axis_index_groups=Y_GROUPS)
    got = lax.all_to_all(part_totals(got), "tm", 0, 0, tiled=True, axis_index_groups=Z_GROUPS)
    pieces, gram = totals(got)
    rhs = lax.all_to_all(pieces, "tm", 0, 0, tiled=True, axis_index_groups=Z_GROUPS)
    weight, inv, scale = operator(gram, variable_factor)
    rhs = rhs.reshape(RANK, PIECE)
    near, far = swapped(*chosen_edges(rhs, EDGE, even))
    even_flag = jnp.where(even, 1, 0).astype(jnp.int32).reshape(1)
    blocks = sweeps(even_flag, rhs, near, far, start, weight, inv, scale)
    blocks = lax.all_to_all(blocks, "tm", 0, 0, tiled=True, axis_index_groups=Y_GROUPS)
    return (time_factor, join(blocks))


def solution(mesh):
    placed_at = (P(None, "tm", "lat"), P(None, "lat"), P(None, "tm"), P(), P(None, "lat"))
    return jax.shard_map(
        per_device,
        mesh=mesh,
        in_specs=placed_at,
        out_specs=(P(None, "tm"), P(None, "lat")),
        check_vma=False,
    )
```

```python
import jax
import jax.numpy as jnp
from jax import lax
from jax.experimental import pallas as pl
from jax.experimental.pallas import tpu as pltpu
from jax.sharding import PartitionSpec as P


RANK = 32
NLON = 360
ROWS = 16
SWEEPS = 8
LANES = 128
PARTS = 4
WIDTH = NLON // PARTS
STRIDE = WIDTH + 14
PIECE = ROWS * STRIDE
HIGHEST = lax.Precision.HIGHEST
F32 = jnp.float32
NT = (((1,), (1,)), ((), ()))

Y_GROUPS = [[y * 4 + z for y in range(4)] for z in range(4)]
Z_GROUPS = [[y * 4 + z for z in range(4)] for y in range(4)]
SWAP_NEAR = [(i, i ^ 1) for i in range(16)]
SWAP_FAR = [(i, (i + 1) % 16 if i % 2 else (i - 1) % 16) for i in range(16)]


def lane_iota(rows):
    return lax.broadcasted_iota(jnp.int32, (rows, LANES), 1)


def row_iota(rows):
    return lax.broadcasted_iota(jnp.int32, (rows, LANES), 0)


def turn(x, shift):
    shift = shift % LANES
    return x if shift == 0 else pltpu.roll(x, shift, axis=1)


def packed(rep, width):
    lane = lane_iota(8)
    total = jnp.zeros((8, LANES), F32)
    for g in range(4):
        here = (lane >= g * width) & (lane < (g + 1) * width)
        total = jnp.where(here, rep[8 * g : 8 * g + 8], total)
    return total


def unpacked(pack, width, at):
    lane = lane_iota(8)
    keep = (lane >= at) & (lane < at + width)
    tiles = [jnp.where(keep, turn(pack, at - g * width), 0.0) for g in range(4)]
    return jnp.concatenate(tiles, axis=0)


PANEL = 4


def eliminated(a):
    row = row_iota(RANK)
    for first in range(0, RANK, PANEL):
        cols = [jnp.broadcast_to(a[:, k : k + 1], (RANK, LANES)) for k in range(first, first + PANEL)]
        for i in range(PANEL):
            k = first + i
            here = row == k
            col = cols[i]
            r = 1.0 / col[k : k + 1, :]
            q = a[k : k + 1, :] * r
            a = jnp.where(here, q, a - col * q)
            for j in range(i + 1, PANEL):
                t = cols[j][k : k + 1, :] * r
                cols[j] = jnp.where(here, t, cols[j] - col * t)
    return a


def split_3(x):
    first = x.astype(jnp.bfloat16)
    rest = x - first.astype(F32)
    second = rest.astype(jnp.bfloat16)
    third = (rest - second.astype(F32)).astype(jnp.bfloat16)
    return first, second, third


def factor_lanes(vf):
    eye = jnp.where(lax.broadcasted_iota(jnp.int32, (RANK, RANK), 0) == lax.broadcasted_iota(jnp.int32, (RANK, RANK), 1), 1.0, 0.0)
    turned = lax.dot_general(eye, vf, NT, precision=HIGHEST, preferred_element_type=F32)
    chosen = jnp.where(lane_iota(8) // 16 == row_iota(8), 1.0, 0.0)
    return jnp.dot(turned, chosen, precision=HIGHEST, preferred_element_type=F32)


TN = (((0,), (0,)), ((), ()))


def gram_lanes(vf):
    chosen = jnp.where(lane_iota(RANK) == row_iota(RANK), 1.0, 0.0)
    wide = jnp.dot(vf, chosen, precision=HIGHEST, preferred_element_type=F32)
    return lax.dot_general(vf, wide, TN, precision=HIGHEST, preferred_element_type=F32)


def project_kernel(data_ref, space_ref, vf_ref, out_ref, acc_ref):
    step = pl.program_id(0)

    @pl.when(step == 0)
    def _():
        acc_ref[...] = jnp.zeros_like(acc_ref)

    space = space_ref[...]
    data = data_ref[...].reshape(LANES, space.shape[1])
    d1, d2, d3 = split_3(data)
    s1, s2, s3 = split_3(space)
    x1 = jnp.concatenate([d1, s1], axis=0)
    x2 = jnp.concatenate([d2, s2], axis=0)
    x3 = jnp.concatenate([d3, s3], axis=0)
    side = jnp.concatenate([s1, s2, s3, s1], axis=0)
    first, mid, last = acc_ref.at[0], acc_ref.at[1], acc_ref.at[2]
    first[...] += lax.dot_general(x1, side, NT, preferred_element_type=F32)
    mid[...] += lax.dot_general(x2, side, NT, preferred_element_type=F32)
    last[...] += lax.dot_general(x3, side, NT, preferred_element_type=F32)

    @pl.when(step == pl.num_programs(0) - 1)
    def _():
        p1, p2, p3 = acc_ref[0], acc_ref[1], acc_ref[2]
        total = p1 + (turn(p1, -32) + p2 + (turn(p1, -64) + turn(p2, -32) + p3))
        rhs = jnp.transpose(total[0:LANES])[0:RANK] * factor_lanes(vf_ref[...])
        for s in (64, 32, 16):
            rhs = rhs + turn(rhs, s)
        gram = jnp.where(lane_iota(RANK) < RANK, total[LANES:], 0.0)
        gram = gram + turn(gram, 32)
        gram = gram + turn(gram, 64)
        g = packed(gram, 32)
        r = packed(rhs, 16)
        for k in range(16):
            out_ref[k, :, 0:128] = g
            out_ref[k, :, 128:256] = r


def project(data, space, vf):
    chunk = 5760
    return pl.pallas_call(
        project_kernel,
        grid=(5760 // chunk,),
        in_specs=[
            pl.BlockSpec((8, 16, chunk), lambda i: (0, 0, i)),
            pl.BlockSpec((RANK, chunk), lambda i: (0, i)),
            pl.BlockSpec((8, RANK), lambda i: (0, 0)),
        ],
        out_specs=pl.BlockSpec((16, 8, 256), lambda i: (0, 0, 0)),
        out_shape=jax.ShapeDtypeStruct((16, 8, 256), F32),
        scratch_shapes=[pltpu.VMEM((3, LANES + RANK, LANES), F32)],
        cost_estimate=pl.CostEstimate(flops=4_000_000_000, bytes_accessed=8_000_000, transcendentals=0),
        name="project",
    )(data, space, vf)


def grant(mebibytes):
    return pltpu.CompilerParams(vmem_limit_bytes=int(mebibytes * 1024 * 1024))


def pack_pieces(pieces, width, store):
    lane = lane_iota(RANK)
    held = None
    for i, piece in enumerate(pieces):
        t, off = divmod(i * width, LANES)
        moved = turn(piece, off)
        value = moved if off == 0 else jnp.where(lane < off, held, moved)
        if off + width >= LANES:
            store(t, value)
            held = moved
        else:
            held = value
    if (i + 1) * width % LANES:
        store((i + 1) * width // LANES, held)


def spot(start):
    return lax.div(start, LANES), lax.rem(start, LANES)


def placed(ref, start, to):
    t, off = divmod(start, LANES)
    lo, hi = ref[:, t * LANES : (t + 1) * LANES], ref[:, (t + 1) * LANES : (t + 2) * LANES]
    return turn(jnp.where(lane_iota(RANK) >= off, lo, hi), to - off)


def window(ref, start):
    count = ref.shape[1] // LANES
    t0, off = start // LANES, start % LANES
    lo = ref[:, t0 * LANES : (t0 + 1) * LANES] if 0 <= t0 < count else None
    t1 = t0 + 1
    hi = ref[:, t1 * LANES : (t1 + 1) * LANES] if off and 0 <= t1 < count else None
    if lo is None:
        return turn(hi, -off)
    if hi is None:
        return turn(lo, -off)
    return turn(jnp.where(lane_iota(ref.shape[0]) >= off, lo, hi), -off)


def tile(t):
    return pl.ds(pl.multiple_of(t * LANES, LANES), LANES)


def hour_kernel(got_ref, stencil_ref, vf_ref, data_ref, tf_ref, out_ref, dbuf, terms, sem):
    copy = pltpu.make_async_copy(data_ref, dbuf, sem)
    copy.start()
    total = got_ref[0]
    for k in range(1, 16):
        total = total + got_ref[k]
    lane = lane_iota(RANK)
    eye = jnp.where(lane == row_iota(RANK), 1.0, 0.0)
    gram = unpacked(total[:, 0:128], 32, 0)
    rhs = unpacked(total[:, 128:256], 16, 32)
    vf = vf_ref[...]
    chosen = jnp.where(lane_iota(16) == row_iota(16) + 32, 1.0, 0.0)
    stencil = lax.dot_general(
        stencil_ref[...], chosen, TN, precision=HIGHEST, preferred_element_type=F32
    )
    a = gram * gram_lanes(vf) + 3.0 * eye + rhs - 0.5 * stencil
    a = eliminated(a)
    tf = jnp.where((lane >= 32) & (lane < 48), a, 0.0)
    tf_ref[...] = turn(tf, -32)[:, 0:16]
    four = jnp.concatenate([tf] * 4, axis=0)
    hour_gram = packed(
        lax.dot_general(tf, four, NT, precision=HIGHEST, preferred_element_type=F32), 32
    )
    rep = tf
    for s in (64, 32, 16):
        rep = rep + turn(rep, s)
    weighted = rep * factor_lanes(vf)
    copy.wait()
    w1, w2, w3 = split_3(weighted)
    w123 = jnp.concatenate([w1, w2, w3], axis=0)
    for c in range(5):
        at = slice(c * 1152, (c + 1) * 1152)
        d1, d2, d3 = split_3(dbuf[:, :, at].reshape(LANES, 1152))
        p1 = jnp.dot(w123, d1, preferred_element_type=F32)
        p2 = jnp.dot(w123[0:64], d2, preferred_element_type=F32)
        p3 = jnp.dot(w1, d3, preferred_element_type=F32)
        terms[:, at] = p1[0:32] + (p1[32:64] + p2[0:32] + (p1[64:96] + p2[32:64] + p3))
    for y in range(PARTS):

        def store(t, value):
            out_ref[y, :, t * LANES : (t + 1) * LANES] = value

        held = None
        for i in range(ROWS):
            t, off = divmod(i * STRIDE, LANES)
            base = i * NLON
            spin = lax.rem(lane + LANES - off, LANES)
            if y == 0:
                moved = placed(terms, base, off + 7)
                moved = jnp.where(spin < 7, placed(terms, base + NLON - 7, off), moved)
            else:
                moved = placed(terms, base + y * WIDTH - 7, off)
            if y == PARTS - 1:
                moved = jnp.where(spin < 97, moved, placed(terms, base, off + 97))
            value = moved if off == 0 else jnp.where(lane < off, held, moved)
            held = value
            if off + STRIDE >= LANES:
                store(t, value)
                held = moved
    for y in range(PARTS):
        out_ref[y, :, PIECE:] = jnp.concatenate([hour_gram] * 4, axis=0)


def hour_mode(got, stencil, vf, data):
    vmem = pl.BlockSpec(memory_space=pltpu.VMEM)
    return pl.pallas_call(
        hour_kernel,
        in_specs=[vmem, vmem, vmem, pl.BlockSpec(memory_space=pl.ANY)],
        out_specs=(vmem, vmem),
        out_shape=(
            jax.ShapeDtypeStruct((RANK, 16), F32),
            jax.ShapeDtypeStruct((PARTS, RANK, PIECE + LANES), F32),
        ),
        scratch_shapes=[
            pltpu.VMEM((8, 16, 5760), F32),
            pltpu.VMEM((RANK, 5760 + LANES), F32),
            pltpu.SemaphoreType.DMA,
        ],
        compiler_params=grant(61.5),
        cost_estimate=pl.CostEstimate(flops=5_000_000_000, bytes_accessed=8_000_000, transcendentals=0),
        name="hour_mode",
    )(got, stencil, vf, data)


def total_kernel(got_ref, piece_ref, gram_ref):
    for c in range(PIECE // LANES + 1):
        at = slice(c * LANES, (c + 1) * LANES)
        total = got_ref[0, :, at]
        for k in range(1, 4):
            total = total + got_ref[k, :, at]
        if c < PIECE // LANES:
            for k in range(4):
                piece_ref[k, :, at] = total
        else:
            gram_ref[...] = total


def part_kernel(got_ref, out_ref):
    for z in range(4):
        for c in range(PIECE // LANES + 1):
            at = slice(c * LANES, (c + 1) * LANES)
            rows = slice(8 * z, 8 * z + 8)
            a, b = got_ref[0, rows, at] + got_ref[1, rows, at], got_ref[2, rows, at] + got_ref[3, rows, at]
            out_ref[z, :, at] = a + b


def part_totals(got):
    vmem = pl.BlockSpec(memory_space=pltpu.VMEM)
    return pl.pallas_call(
        part_kernel,
        in_specs=[vmem],
        out_specs=vmem,
        out_shape=jax.ShapeDtypeStruct((4, 8, PIECE + LANES), F32),
        compiler_params=grant(8),
        name="part_totals",
    )(got)


def totals(got):
    vmem = pl.BlockSpec(memory_space=pltpu.VMEM)
    return pl.pallas_call(
        total_kernel,
        in_specs=[vmem],
        out_specs=(vmem, vmem),
        out_shape=(
            jax.ShapeDtypeStruct((4, 8, PIECE), F32),
            jax.ShapeDtypeStruct((8, LANES), F32),
        ),
        compiler_params=grant(8),
        name="totals",
    )(got)


def operator_kernel(gram_ref, vf_ref, weight_ref, inv_ref, scale_ref):
    lane = lane_iota(RANK)
    row = row_iota(RANK)
    on_diag = lane == row
    gram = unpacked(gram_ref[...], 32, 0)
    diag = jnp.where(on_diag, gram, 0.0)
    scale_col = jnp.sqrt(jnp.sum(diag, axis=1, keepdims=True) + 1e-06)
    scale_row = jnp.sqrt(jnp.sum(diag, axis=0, keepdims=True) + 1e-06)
    op = gram / (scale_col * scale_row) * gram_lanes(vf_ref[...]) + 2.0 * jnp.where(on_diag, 1.0, 0.0)
    a = eliminated(op + jnp.where(lane == row + 32, 1.0, 0.0))
    inv = jnp.where((lane >= 32) & (lane < 64), a, 0.0)
    half = 0.5 * inv
    high = half.astype(jnp.bfloat16).astype(F32)
    low = half - high
    weight = turn(high, -32) + high + turn(low, 32) + turn(low, 64)
    weight_ref[...] = weight.astype(jnp.bfloat16)
    i1, i2, i3 = (part.astype(F32) for part in split_3(inv))
    inv_ref[:, 0:128] = (turn(i1, -32) + i1 + turn(i1, 32) + turn(i2, 64)).astype(jnp.bfloat16)
    inv_ref[:, 128:256] = (turn(i2, -32) + i3).astype(jnp.bfloat16)
    scale_ref[...] = jnp.broadcast_to(scale_col, (RANK, LANES))


def operator(gram, vf):
    vmem = pl.BlockSpec(memory_space=pltpu.VMEM)
    return pl.pallas_call(
        operator_kernel,
        in_specs=[vmem, vmem],
        out_specs=(vmem, vmem, vmem),
        out_shape=(
            jax.ShapeDtypeStruct((RANK, LANES), jnp.bfloat16),
            jax.ShapeDtypeStruct((RANK, 2 * LANES), jnp.bfloat16),
            jax.ShapeDtypeStruct((RANK, LANES), F32),
        ),
        name="operator",
        compiler_params=grant(4),
        cost_estimate=pl.CostEstimate(flops=4_000_000_000, bytes_accessed=100_000, transcendentals=0),
    )(gram, vf)


EXT = ROWS + 16
EDGE = 6 * LANES


def sweep_kernel(
    even_ref, rhs_ref, near_ref, far_ref, start_ref, weight_ref, inv_ref, scale_ref, out_ref, state, base, codes
):
    even = even_ref[0] == 1
    scale = scale_ref[...]
    inv = inv_ref[:, 0 : 6 * RANK]
    for i in range(1, EXT - 1):
        at = slice(i * LANES, (i + 1) * LANES)
        if i < 8:
            first = (i + 8) * STRIDE - (PIECE - EDGE) - 1
            v = jnp.where(even, window(far_ref, first), window(near_ref, first))
        elif i < 8 + ROWS:
            v = window(rhs_ref, (i - 8) * STRIDE - 1)
        else:
            first = (i - 24) * STRIDE - 1
            v = jnp.where(even, window(near_ref, first), window(far_ref, first))
        state[:, at] = v / scale
    for c in range(EXT // 2):
        at = slice(max(1, 2 * c) * LANES, min(EXT - 1, 2 * c + 2) * LANES)
        x1, x2, x3 = split_3(state[:, at])
        x6 = jnp.concatenate([x1, x2, x3, x1, x2, x1], axis=0)
        base[:, at] = jnp.dot(inv, x6, preferred_element_type=F32)
    for i in range(EXT):
        at = slice(i * LANES, (i + 1) * LANES)
        state[:, at] = start_ref[0:RANK, at]
        codes[0:8, at] = jnp.broadcast_to(start_ref[RANK : RANK + 1, at], (8, LANES))
        codes[8:16, at] = jnp.broadcast_to(start_ref[RANK + 1 : RANK + 2, at], (8, LANES))
    weight = weight_ref[...]

    def line(i):
        at = slice(i * LANES, (i + 1) * LANES)
        tiles = [state[8 * g : 8 * g + 8, at] for g in range(4)]
        return [(turn(c, -1), c, turn(c, 1)) for c in tiles]

    for step in range(SWEEPS):
        low_row, high_row = 1 + step, EXT - 1 - step
        before, here = line(low_row - 1), line(low_row)
        for i in range(low_row, high_row):
            at = slice(i * LANES, (i + 1) * LANES)
            after = line(i + 1)
            picks = [[codes[8 * d : 8 * d + 8, at] == k for k in (1.0, 2.0, 3.0)] for d in range(2)]

            def pick(d, triple):
                ahead, same, behind = triple
                same_at, ahead_at, behind_at = picks[d]
                rest = jnp.where(same_at, same, 0.0)
                return jnp.where(ahead_at, ahead, jnp.where(behind_at, behind, rest))

            near = jnp.concatenate(
                [
                    (here[g][0] + here[g][2]) + (pick(0, before[g]) + pick(1, after[g]))
                    for g in range(4)
                ],
                axis=0,
            )
            if (i - low_row) % 2 == 0:
                first = near
            else:
                pair = jnp.concatenate([first, near], axis=1)
                last = (i + 1) * LANES
                done = slice(last - pair.shape[1], last)
                high = pair.astype(jnp.bfloat16)
                low = (pair - high.astype(F32)).astype(jnp.bfloat16)
                x4 = jnp.concatenate([high, low, high, low], axis=0)
                state[:, done] = base[:, done] + jnp.dot(weight, x4, preferred_element_type=F32)
            before, here = here, after

    def store(t, value):
        for k in range(PARTS):
            out_ref[k, :, t * LANES : (t + 1) * LANES] = value

    pack_pieces(
        [turn(state[:, (8 + i) * LANES : (9 + i) * LANES], -8) for i in range(ROWS)], WIDTH, store
    )


def sweeps(even, rhs, near, far, start, weight, inv, scale):
    vmem = pl.BlockSpec(memory_space=pltpu.VMEM)
    return pl.pallas_call(
        sweep_kernel,
        in_specs=[pl.BlockSpec(memory_space=pltpu.SMEM)] + [vmem] * 7,
        out_specs=vmem,
        out_shape=jax.ShapeDtypeStruct((PARTS, RANK, 12 * LANES), F32),
        scratch_shapes=[
            pltpu.VMEM((RANK, EXT * LANES), F32),
            pltpu.VMEM((RANK, EXT * LANES), F32),
            pltpu.VMEM((16, EXT * LANES), F32),
        ],
        compiler_params=grant(12),
        name="sweeps",
    )(even, rhs, near, far, start, weight, inv, scale)


def join_kernel(got_ref, out_ref):
    lane = lane_iota(RANK)

    def row(i, held):
        for y in range(PARTS):
            to_tile, off = spot(i * NLON + y * WIDTH)
            first, at = spot(i * WIDTH)
            joint = jnp.where(lane >= at, got_ref[y, :, tile(first)], got_ref[y, :, tile(first + 1)])
            moved = pltpu.roll(joint, lax.rem(off + LANES - at, LANES), axis=1)
            value = jnp.where(lane < off, held, moved)
            out_ref[:, tile(to_tile)] = value
            held = jnp.where(off + WIDTH >= LANES, moved, value)
        return held

    lax.fori_loop(0, ROWS, row, jnp.zeros((RANK, LANES), F32), unroll=16)


def join(got):
    vmem = pl.BlockSpec(memory_space=pltpu.VMEM)
    return pl.pallas_call(
        join_kernel,
        in_specs=[vmem],
        out_specs=vmem,
        out_shape=jax.ShapeDtypeStruct((RANK, ROWS * NLON), F32),
        compiler_params=grant(8),
        name="join",
    )(got)


def link_codes(links):
    column = jnp.arange(links.shape[1], dtype=jnp.int32) % NLON
    target = (links % NLON - column + NLON) % NLON
    code = jnp.where(target == 1, 2.0, jnp.where(target == NLON - 1, 3.0, 1.0))
    return jnp.where(links >= 0, code, 0.0).astype(F32)


def swapped(edge_near, edge_far):
    far = lax.ppermute(edge_far, "lat", SWAP_FAR)
    near = lax.ppermute(edge_near, "lat", SWAP_NEAR)
    return near, far


def chosen_edges(block, width, even):
    top, bottom = block[:, :width], block[:, block.shape[1] - width :]
    return jnp.where(even, bottom, top), jnp.where(even, top, bottom)


def per_device(data, space_init, time_init, variable_factor, neighbours):
    tm = lax.axis_index("tm")
    lat = lax.axis_index("lat")
    even = lat % 2 == 0
    part = tm // 4

    hours = time_init.T
    low = lax.ppermute(hours, "tm", [(i, (i + 1) % 16) for i in range(16)])
    high = lax.ppermute(hours, "tm", [((i + 1) % 16, i) for i in range(16)])
    sums = project(data, space_init, variable_factor)
    got = lax.all_to_all(sums, "lat", 0, 0, tiled=True)

    low = jnp.where(tm == 0, 0.0, low[-2:])
    high = jnp.where(tm == 15, 0.0, high[:2])
    padded = jnp.concatenate([low, hours, high], axis=0)
    stencil = padded[:-4] - 4.0 * padded[1:-3] - 4.0 * padded[3:-1] + padded[4:]

    own = jnp.concatenate([space_init, link_codes(neighbours[2:4])], axis=0)
    own, _ = lax.optimization_barrier((own, sums[0, 0, 0]))
    own = own.reshape(RANK + 2, ROWS, NLON)
    own = jnp.concatenate([own[:, :, NLON - 8 :], own, own[:, :, :30]], axis=2)
    own = lax.dynamic_slice_in_dim(own, part * WIDTH, LANES, axis=2)
    own = own.reshape(RANK + 2, ROWS * LANES)
    to_near, to_far = chosen_edges(own, 8 * LANES, even)
    to_near, to_far, got = lax.optimization_barrier((to_near, to_far, got))
    start_near, start_far = swapped(to_near, to_far)
    start = jnp.concatenate(
        [
            jnp.where(even, start_far, start_near),
            own,
            jnp.where(even, start_near, start_far),
        ],
        axis=1,
    )

    time_factor, terms = hour_mode(got, stencil, variable_factor, data)
    got = lax.all_to_all(terms, "tm", 0, 0, tiled=True, axis_index_groups=Y_GROUPS)
    got = lax.all_to_all(part_totals(got), "tm", 0, 0, tiled=True, axis_index_groups=Z_GROUPS)
    pieces, gram = totals(got)
    rhs = lax.all_to_all(pieces, "tm", 0, 0, tiled=True, axis_index_groups=Z_GROUPS)
    weight, inv, scale = operator(gram, variable_factor)
    rhs = rhs.reshape(RANK, PIECE)
    near, far = swapped(*chosen_edges(rhs, EDGE, even))
    even_flag = jnp.where(even, 1, 0).astype(jnp.int32).reshape(1)
    blocks = sweeps(even_flag, rhs, near, far, start, weight, inv, scale)
    blocks = lax.all_to_all(blocks, "tm", 0, 0, tiled=True, axis_index_groups=Y_GROUPS)
    return (time_factor, join(blocks))


def solution(mesh):
    placed_at = (P(None, "tm", "lat"), P(None, "lat"), P(None, "tm"), P(), P(None, "lat"))
    return jax.shard_map(
        per_device,
        mesh=mesh,
        in_specs=placed_at,
        out_specs=(P(None, "tm"), P(None, "lat")),
        check_vma=False,
    )
```

```python
import jax
import jax.numpy as jnp
from jax import lax
from jax.experimental import pallas as pl
from jax.experimental.pallas import tpu as pltpu
from jax.sharding import PartitionSpec as P


RANK = 32
NLON = 360
ROWS = 16
SWEEPS = 8
LANES = 128
PARTS = 4
WIDTH = NLON // PARTS
STRIDE = WIDTH + 14
PIECE = ROWS * STRIDE
HIGHEST = lax.Precision.HIGHEST
F32 = jnp.float32
NT = (((1,), (1,)), ((), ()))

Y_GROUPS = [[y * 4 + z for y in range(4)] for z in range(4)]
Z_GROUPS = [[y * 4 + z for z in range(4)] for y in range(4)]
SWAP_NEAR = [(i, i ^ 1) for i in range(16)]
SWAP_FAR = [(i, (i + 1) % 16 if i % 2 else (i - 1) % 16) for i in range(16)]


def lane_iota(rows):
    return lax.broadcasted_iota(jnp.int32, (rows, LANES), 1)


def row_iota(rows):
    return lax.broadcasted_iota(jnp.int32, (rows, LANES), 0)


def turn(x, shift):
    shift = shift % LANES
    return x if shift == 0 else pltpu.roll(x, shift, axis=1)


def packed(rep, width):
    lane = lane_iota(8)
    total = jnp.zeros((8, LANES), F32)
    for g in range(4):
        here = (lane >= g * width) & (lane < (g + 1) * width)
        total = jnp.where(here, rep[8 * g : 8 * g + 8], total)
    return total


def unpacked(pack, width, at):
    lane = lane_iota(8)
    keep = (lane >= at) & (lane < at + width)
    tiles = [jnp.where(keep, turn(pack, at - g * width), 0.0) for g in range(4)]
    return jnp.concatenate(tiles, axis=0)


PANEL = 4


def eliminated(a):
    row = row_iota(RANK)
    for first in range(0, RANK, PANEL):
        cols = [jnp.broadcast_to(a[:, k : k + 1], (RANK, LANES)) for k in range(first, first + PANEL)]
        for i in range(PANEL):
            k = first + i
            here = row == k
            col = cols[i]
            r = 1.0 / col[k : k + 1, :]
            q = a[k : k + 1, :] * r
            a = jnp.where(here, q, a - col * q)
            for j in range(i + 1, PANEL):
                t = cols[j][k : k + 1, :] * r
                cols[j] = jnp.where(here, t, cols[j] - col * t)
    return a


def split_3(x):
    first = x.astype(jnp.bfloat16)
    rest = x - first.astype(F32)
    second = rest.astype(jnp.bfloat16)
    third = (rest - second.astype(F32)).astype(jnp.bfloat16)
    return first, second, third


def factor_lanes(vf):
    eye = jnp.where(lax.broadcasted_iota(jnp.int32, (RANK, RANK), 0) == lax.broadcasted_iota(jnp.int32, (RANK, RANK), 1), 1.0, 0.0)
    turned = lax.dot_general(eye, vf, NT, precision=HIGHEST, preferred_element_type=F32)
    chosen = jnp.where(lane_iota(8) // 16 == row_iota(8), 1.0, 0.0)
    return jnp.dot(turned, chosen, precision=HIGHEST, preferred_element_type=F32)


TN = (((0,), (0,)), ((), ()))


def gram_lanes(vf):
    chosen = jnp.where(lane_iota(RANK) == row_iota(RANK), 1.0, 0.0)
    wide = jnp.dot(vf, chosen, precision=HIGHEST, preferred_element_type=F32)
    return lax.dot_general(vf, wide, TN, precision=HIGHEST, preferred_element_type=F32)


def project_kernel(data_ref, space_ref, vf_ref, out_ref, acc_ref):
    step = pl.program_id(0)

    @pl.when(step == 0)
    def _():
        acc_ref[...] = jnp.zeros_like(acc_ref)

    space = space_ref[...]
    data = data_ref[...].reshape(LANES, space.shape[1])
    d1, d2, d3 = split_3(data)
    s1, s2, s3 = split_3(space)
    x1 = jnp.concatenate([d1, s1], axis=0)
    x2 = jnp.concatenate([d2, s2], axis=0)
    x3 = jnp.concatenate([d3, s3], axis=0)
    side = jnp.concatenate([s1, s2, s3, s1], axis=0)
    first, mid, last = acc_ref.at[0], acc_ref.at[1], acc_ref.at[2]
    first[...] += lax.dot_general(x1, side, NT, preferred_element_type=F32)
    mid[...] += lax.dot_general(x2, side, NT, preferred_element_type=F32)
    last[...] += lax.dot_general(x3, side, NT, preferred_element_type=F32)

    @pl.when(step == pl.num_programs(0) - 1)
    def _():
        p1, p2, p3 = acc_ref[0], acc_ref[1], acc_ref[2]
        total = p1 + (turn(p1, -32) + p2 + (turn(p1, -64) + turn(p2, -32) + p3))
        rhs = jnp.transpose(total[0:LANES])[0:RANK] * factor_lanes(vf_ref[...])
        for s in (64, 32, 16):
            rhs = rhs + turn(rhs, s)
        gram = jnp.where(lane_iota(RANK) < RANK, total[LANES:], 0.0)
        gram = gram + turn(gram, 32)
        gram = gram + turn(gram, 64)
        g = packed(gram, 32)
        r = packed(rhs, 16)
        for k in range(16):
            out_ref[k, :, 0:128] = g
            out_ref[k, :, 128:256] = r


def project(data, space, vf):
    chunk = 5760
    return pl.pallas_call(
        project_kernel,
        grid=(5760 // chunk,),
        in_specs=[
            pl.BlockSpec((8, 16, chunk), lambda i: (0, 0, i)),
            pl.BlockSpec((RANK, chunk), lambda i: (0, i)),
            pl.BlockSpec((8, RANK), lambda i: (0, 0)),
        ],
        out_specs=pl.BlockSpec((16, 8, 256), lambda i: (0, 0, 0)),
        out_shape=jax.ShapeDtypeStruct((16, 8, 256), F32),
        scratch_shapes=[pltpu.VMEM((3, LANES + RANK, LANES), F32)],
        cost_estimate=pl.CostEstimate(flops=4_000_000_000, bytes_accessed=8_000_000, transcendentals=0),
        name="project",
    )(data, space, vf)


def grant(mebibytes):
    return pltpu.CompilerParams(vmem_limit_bytes=int(mebibytes * 1024 * 1024))


def pack_pieces(pieces, width, store):
    lane = lane_iota(RANK)
    held = None
    for i, piece in enumerate(pieces):
        t, off = divmod(i * width, LANES)
        moved = turn(piece, off)
        value = moved if off == 0 else jnp.where(lane < off, held, moved)
        if off + width >= LANES:
            store(t, value)
            held = moved
        else:
            held = value
    if (i + 1) * width % LANES:
        store((i + 1) * width // LANES, held)


def placed(ref, start, to):
    t, off = divmod(start, LANES)
    lo, hi = ref[:, t * LANES : (t + 1) * LANES], ref[:, (t + 1) * LANES : (t + 2) * LANES]
    return turn(jnp.where(lane_iota(RANK) >= off, lo, hi), to - off)


def window(ref, start):
    count = ref.shape[1] // LANES
    t0, off = start // LANES, start % LANES
    lo = ref[:, t0 * LANES : (t0 + 1) * LANES] if 0 <= t0 < count else None
    t1 = t0 + 1
    hi = ref[:, t1 * LANES : (t1 + 1) * LANES] if off and 0 <= t1 < count else None
    if lo is None:
        return turn(hi, -off)
    if hi is None:
        return turn(lo, -off)
    return turn(jnp.where(lane_iota(ref.shape[0]) >= off, lo, hi), -off)


def hour_kernel(got_ref, stencil_ref, vf_ref, data_ref, tf_ref, out_ref, dbuf, terms, sem):
    copy = pltpu.make_async_copy(data_ref, dbuf, sem)
    copy.start()
    total = got_ref[0]
    for k in range(1, 16):
        total = total + got_ref[k]
    lane = lane_iota(RANK)
    eye = jnp.where(lane == row_iota(RANK), 1.0, 0.0)
    gram = unpacked(total[:, 0:128], 32, 0)
    rhs = unpacked(total[:, 128:256], 16, 32)
    vf = vf_ref[...]
    chosen = jnp.where(lane_iota(16) == row_iota(16) + 32, 1.0, 0.0)
    stencil = lax.dot_general(
        stencil_ref[...], chosen, TN, precision=HIGHEST, preferred_element_type=F32
    )
    a = gram * gram_lanes(vf) + 3.0 * eye + rhs - 0.5 * stencil
    a = eliminated(a)
    tf = jnp.where((lane >= 32) & (lane < 48), a, 0.0)
    tf_ref[...] = turn(tf, -32)[:, 0:16]
    four = jnp.concatenate([tf] * 4, axis=0)
    hour_gram = packed(
        lax.dot_general(tf, four, NT, precision=HIGHEST, preferred_element_type=F32), 32
    )
    rep = tf
    for s in (64, 32, 16):
        rep = rep + turn(rep, s)
    weighted = rep * factor_lanes(vf)
    copy.wait()
    w1, w2, w3 = split_3(weighted)
    w123 = jnp.concatenate([w1, w2, w3], axis=0)
    for c in range(5):
        at = slice(c * 1152, (c + 1) * 1152)
        d1, d2, d3 = split_3(dbuf[:, :, at].reshape(LANES, 1152))
        p1 = jnp.dot(w123, d1, preferred_element_type=F32)
        p2 = jnp.dot(w123[0:64], d2, preferred_element_type=F32)
        p3 = jnp.dot(w1, d3, preferred_element_type=F32)
        terms[:, at] = p1[0:32] + (p1[32:64] + p2[0:32] + (p1[64:96] + p2[32:64] + p3))
    for y in range(PARTS):

        def store(t, value):
            out_ref[y, :, t * LANES : (t + 1) * LANES] = value

        held = None
        for i in range(ROWS):
            t, off = divmod(i * STRIDE, LANES)
            base = i * NLON
            spin = lax.rem(lane + LANES - off, LANES)
            if y == 0:
                moved = placed(terms, base, off + 7)
                moved = jnp.where(spin < 7, placed(terms, base + NLON - 7, off), moved)
            else:
                moved = placed(terms, base + y * WIDTH - 7, off)
            if y == PARTS - 1:
                moved = jnp.where(spin < 97, moved, placed(terms, base, off + 97))
            value = moved if off == 0 else jnp.where(lane < off, held, moved)
            held = value
            if off + STRIDE >= LANES:
                store(t, value)
                held = moved
    for y in range(PARTS):
        out_ref[y, :, PIECE:] = jnp.concatenate([hour_gram] * 4, axis=0)


def hour_mode(got, stencil, vf, data):
    vmem = pl.BlockSpec(memory_space=pltpu.VMEM)
    return pl.pallas_call(
        hour_kernel,
        in_specs=[vmem, vmem, vmem, pl.BlockSpec(memory_space=pl.ANY)],
        out_specs=(vmem, vmem),
        out_shape=(
            jax.ShapeDtypeStruct((RANK, 16), F32),
            jax.ShapeDtypeStruct((PARTS, RANK, PIECE + LANES), F32),
        ),
        scratch_shapes=[
            pltpu.VMEM((8, 16, 5760), F32),
            pltpu.VMEM((RANK, 5760 + LANES), F32),
            pltpu.SemaphoreType.DMA,
        ],
        compiler_params=grant(61.5),
        cost_estimate=pl.CostEstimate(flops=5_000_000_000, bytes_accessed=8_000_000, transcendentals=0),
        name="hour_mode",
    )(got, stencil, vf, data)


def total_kernel(got_ref, piece_ref, gram_ref):
    for c in range(PIECE // LANES + 1):
        at = slice(c * LANES, (c + 1) * LANES)
        total = got_ref[0, :, at]
        for k in range(1, 4):
            total = total + got_ref[k, :, at]
        if c < PIECE // LANES:
            for k in range(4):
                piece_ref[k, :, at] = total
        else:
            gram_ref[...] = total


def part_kernel(got_ref, out_ref):
    for z in range(4):
        for c in range(PIECE // LANES + 1):
            at = slice(c * LANES, (c + 1) * LANES)
            rows = slice(8 * z, 8 * z + 8)
            a, b = got_ref[0, rows, at] + got_ref[1, rows, at], got_ref[2, rows, at] + got_ref[3, rows, at]
            out_ref[z, :, at] = a + b


def part_totals(got):
    vmem = pl.BlockSpec(memory_space=pltpu.VMEM)
    return pl.pallas_call(
        part_kernel,
        in_specs=[vmem],
        out_specs=vmem,
        out_shape=jax.ShapeDtypeStruct((4, 8, PIECE + LANES), F32),
        compiler_params=grant(8),
        name="part_totals",
    )(got)


def totals(got):
    vmem = pl.BlockSpec(memory_space=pltpu.VMEM)
    return pl.pallas_call(
        total_kernel,
        in_specs=[vmem],
        out_specs=(vmem, vmem),
        out_shape=(
            jax.ShapeDtypeStruct((4, 8, PIECE), F32),
            jax.ShapeDtypeStruct((8, LANES), F32),
        ),
        compiler_params=grant(8),
        name="totals",
    )(got)


def operator_kernel(gram_ref, vf_ref, weight_ref, inv_ref, scale_ref):
    lane = lane_iota(RANK)
    row = row_iota(RANK)
    on_diag = lane == row
    gram = unpacked(gram_ref[...], 32, 0)
    diag = jnp.where(on_diag, gram, 0.0)
    scale_col = jnp.sqrt(jnp.sum(diag, axis=1, keepdims=True) + 1e-06)
    scale_row = jnp.sqrt(jnp.sum(diag, axis=0, keepdims=True) + 1e-06)
    op = gram / (scale_col * scale_row) * gram_lanes(vf_ref[...]) + 2.0 * jnp.where(on_diag, 1.0, 0.0)
    a = eliminated(op + jnp.where(lane == row + 32, 1.0, 0.0))
    inv = jnp.where((lane >= 32) & (lane < 64), a, 0.0)
    half = 0.5 * inv
    high = half.astype(jnp.bfloat16).astype(F32)
    low = half - high
    weight = turn(high, -32) + high + turn(low, 32) + turn(low, 64)
    weight_ref[...] = weight.astype(jnp.bfloat16)
    i1, i2, i3 = (part.astype(F32) for part in split_3(inv))
    inv_ref[:, 0:128] = (turn(i1, -32) + i1 + turn(i1, 32) + turn(i2, 64)).astype(jnp.bfloat16)
    inv_ref[:, 128:256] = (turn(i2, -32) + i3).astype(jnp.bfloat16)
    scale_ref[...] = jnp.broadcast_to(scale_col, (RANK, LANES))


def operator(gram, vf):
    vmem = pl.BlockSpec(memory_space=pltpu.VMEM)
    return pl.pallas_call(
        operator_kernel,
        in_specs=[vmem, vmem],
        out_specs=(vmem, vmem, vmem),
        out_shape=(
            jax.ShapeDtypeStruct((RANK, LANES), jnp.bfloat16),
            jax.ShapeDtypeStruct((RANK, 2 * LANES), jnp.bfloat16),
            jax.ShapeDtypeStruct((RANK, LANES), F32),
        ),
        name="operator",
        compiler_params=grant(4),
        cost_estimate=pl.CostEstimate(flops=4_000_000_000, bytes_accessed=100_000, transcendentals=0),
    )(gram, vf)


EXT = ROWS + 16
EDGE = 6 * LANES


def sweep_kernel(
    even_ref, rhs_ref, near_ref, far_ref, start_ref, weight_ref, inv_ref, scale_ref, out_ref, state, base, codes
):
    even = even_ref[0] == 1
    scale = scale_ref[...]
    inv = inv_ref[:, 0 : 6 * RANK]
    for i in range(1, EXT - 1):
        at = slice(i * LANES, (i + 1) * LANES)
        if i < 8:
            first = (i + 8) * STRIDE - (PIECE - EDGE) - 1
            v = jnp.where(even, window(far_ref, first), window(near_ref, first))
        elif i < 8 + ROWS:
            v = window(rhs_ref, (i - 8) * STRIDE - 1)
        else:
            first = (i - 24) * STRIDE - 1
            v = jnp.where(even, window(near_ref, first), window(far_ref, first))
        state[:, at] = v / scale
    for c in range(EXT // 2):
        at = slice(max(1, 2 * c) * LANES, min(EXT - 1, 2 * c + 2) * LANES)
        x1, x2, x3 = split_3(state[:, at])
        x6 = jnp.concatenate([x1, x2, x3, x1, x2, x1], axis=0)
        base[:, at] = jnp.dot(inv, x6, preferred_element_type=F32)
    for i in range(EXT):
        at = slice(i * LANES, (i + 1) * LANES)
        state[:, at] = start_ref[0:RANK, at]
        codes[0:8, at] = jnp.broadcast_to(start_ref[RANK : RANK + 1, at], (8, LANES))
        codes[8:16, at] = jnp.broadcast_to(start_ref[RANK + 1 : RANK + 2, at], (8, LANES))
    weight = weight_ref[...]

    def line(i):
        at = slice(i * LANES, (i + 1) * LANES)
        tiles = [state[8 * g : 8 * g + 8, at] for g in range(4)]
        return [(turn(c, -1), c, turn(c, 1)) for c in tiles]

    for step in range(SWEEPS):
        low_row, high_row = 1 + step, EXT - 1 - step
        before, here = line(low_row - 1), line(low_row)
        for i in range(low_row, high_row):
            at = slice(i * LANES, (i + 1) * LANES)
            after = line(i + 1)
            picks = [[codes[8 * d : 8 * d + 8, at] == k for k in (1.0, 2.0, 3.0)] for d in range(2)]

            def pick(d, triple):
                ahead, same, behind = triple
                same_at, ahead_at, behind_at = picks[d]
                rest = jnp.where(same_at, same, 0.0)
                return jnp.where(ahead_at, ahead, jnp.where(behind_at, behind, rest))

            near = jnp.concatenate(
                [
                    (here[g][0] + here[g][2]) + (pick(0, before[g]) + pick(1, after[g]))
                    for g in range(4)
                ],
                axis=0,
            )
            if (i - low_row) % 2 == 0:
                first = near
            else:
                pair = jnp.concatenate([first, near], axis=1)
                last = (i + 1) * LANES
                done = slice(last - pair.shape[1], last)
                high = pair.astype(jnp.bfloat16)
                low = (pair - high.astype(F32)).astype(jnp.bfloat16)
                x4 = jnp.concatenate([high, low, high, low], axis=0)
                state[:, done] = base[:, done] + jnp.dot(weight, x4, preferred_element_type=F32)
            before, here = here, after

    def store(t, value):
        groups = [value[8 * g : 8 * g + 8] for g in range(4)]
        if t == 11:
            lane = lane_iota(8)
            joint = groups[0]
            for g in range(1, 4):
                joint = jnp.where(lane >= 32 * g, turn(groups[g], 32 * g), joint)
            groups = [joint]
        for k in range(PARTS):
            for g, group in enumerate(groups):
                out_ref[k, 32 * t + 8 * g : 32 * t + 8 * g + 8, :] = group

    pack_pieces(
        [turn(state[:, (8 + i) * LANES : (9 + i) * LANES], -8) for i in range(ROWS)], WIDTH, store
    )


def sweeps(even, rhs, near, far, start, weight, inv, scale):
    vmem = pl.BlockSpec(memory_space=pltpu.VMEM)
    return pl.pallas_call(
        sweep_kernel,
        in_specs=[pl.BlockSpec(memory_space=pltpu.SMEM)] + [vmem] * 7,
        out_specs=vmem,
        out_shape=jax.ShapeDtypeStruct((PARTS, 360, LANES), F32),
        scratch_shapes=[
            pltpu.VMEM((RANK, EXT * LANES), F32),
            pltpu.VMEM((RANK, EXT * LANES), F32),
            pltpu.VMEM((16, EXT * LANES), F32),
        ],
        compiler_params=grant(12),
        name="sweeps",
    )(even, rhs, near, far, start, weight, inv, scale)


def join_kernel(got_ref, out_ref):
    lane = lane_iota(RANK)

    def read(y, t):
        if t < 11:
            return got_ref[y, 32 * t : 32 * t + 32, :]
        last = got_ref[y, 352:360, :]
        return jnp.concatenate([turn(last, -32 * g) for g in range(4)], axis=0)

    held = None
    for i in range(ROWS):
        for y in range(PARTS):
            to_tile, off = divmod(i * NLON + y * WIDTH, LANES)
            first, at = divmod(i * WIDTH, LANES)
            joint = read(y, first)
            if at + WIDTH > LANES:
                joint = jnp.where(lane >= at, joint, read(y, first + 1))
            moved = turn(joint, off - at)
            value = moved if off == 0 else jnp.where(lane < off, held, moved)
            held = value
            if off + WIDTH >= LANES:
                out_ref[:, to_tile * LANES : (to_tile + 1) * LANES] = value
                held = moved


def join(got):
    vmem = pl.BlockSpec(memory_space=pltpu.VMEM)
    return pl.pallas_call(
        join_kernel,
        in_specs=[vmem],
        out_specs=vmem,
        out_shape=jax.ShapeDtypeStruct((RANK, ROWS * NLON), F32),
        compiler_params=grant(8),
        name="join",
    )(got)


def link_codes(links):
    column = jnp.arange(links.shape[1], dtype=jnp.int32) % NLON
    target = (links % NLON - column + NLON) % NLON
    code = jnp.where(target == 1, 2.0, jnp.where(target == NLON - 1, 3.0, 1.0))
    return jnp.where(links >= 0, code, 0.0).astype(F32)


def swapped(edge_near, edge_far):
    far = lax.ppermute(edge_far, "lat", SWAP_FAR)
    near = lax.ppermute(edge_near, "lat", SWAP_NEAR)
    return near, far


def chosen_edges(block, width, even):
    top, bottom = block[:, :width], block[:, block.shape[1] - width :]
    return jnp.where(even, bottom, top), jnp.where(even, top, bottom)


def per_device(data, space_init, time_init, variable_factor, neighbours):
    tm = lax.axis_index("tm")
    lat = lax.axis_index("lat")
    even = lat % 2 == 0
    part = tm // 4

    hours = time_init.T
    low = lax.ppermute(hours, "tm", [(i, (i + 1) % 16) for i in range(16)])
    high = lax.ppermute(hours, "tm", [((i + 1) % 16, i) for i in range(16)])
    sums = project(data, space_init, variable_factor)
    got = lax.all_to_all(sums, "lat", 0, 0, tiled=True)

    low = jnp.where(tm == 0, 0.0, low[-2:])
    high = jnp.where(tm == 15, 0.0, high[:2])
    padded = jnp.concatenate([low, hours, high], axis=0)
    stencil = padded[:-4] - 4.0 * padded[1:-3] - 4.0 * padded[3:-1] + padded[4:]

    own = jnp.concatenate([space_init, link_codes(neighbours[2:4])], axis=0)
    own, _ = lax.optimization_barrier((own, sums[0, 0, 0]))
    own = own.reshape(RANK + 2, ROWS, NLON)
    own = jnp.concatenate([own[:, :, NLON - 8 :], own, own[:, :, :30]], axis=2)
    own = lax.dynamic_slice_in_dim(own, part * WIDTH, LANES, axis=2)
    own = own.reshape(RANK + 2, ROWS * LANES)
    to_near, to_far = chosen_edges(own, 8 * LANES, even)
    to_near, to_far, got = lax.optimization_barrier((to_near, to_far, got))
    start_near, start_far = swapped(to_near, to_far)
    start = jnp.concatenate(
        [
            jnp.where(even, start_far, start_near),
            own,
            jnp.where(even, start_near, start_far),
        ],
        axis=1,
    )

    time_factor, terms = hour_mode(got, stencil, variable_factor, data)
    got = lax.all_to_all(terms, "tm", 0, 0, tiled=True, axis_index_groups=Y_GROUPS)
    got = lax.all_to_all(part_totals(got), "tm", 0, 0, tiled=True, axis_index_groups=Z_GROUPS)
    pieces, gram = totals(got)
    rhs = lax.all_to_all(pieces, "tm", 0, 0, tiled=True, axis_index_groups=Z_GROUPS)
    weight, inv, scale = operator(gram, variable_factor)
    rhs = rhs.reshape(RANK, PIECE)
    near, far = swapped(*chosen_edges(rhs, EDGE, even))
    even_flag = jnp.where(even, 1, 0).astype(jnp.int32).reshape(1)
    blocks = sweeps(even_flag, rhs, near, far, start, weight, inv, scale)
    blocks = lax.all_to_all(blocks, "tm", 0, 0, tiled=True, axis_index_groups=Y_GROUPS)
    return (time_factor, join(blocks))


def solution(mesh):
    placed_at = (P(None, "tm", "lat"), P(None, "lat"), P(None, "tm"), P(), P(None, "lat"))
    return jax.shard_map(
        per_device,
        mesh=mesh,
        in_specs=placed_at,
        out_specs=(P(None, "tm"), P(None, "lat")),
        check_vma=False,
    )
```
